512 devices in a mesh: dp: 4 (over y), expert: 128 (over x, z, core).
Axes of the slice: x: 4, y: 4, z: 16, core: 2. Of those that a mesh axis runs over, the one named last changes fastest.
Arguments:
- tokens: bfloat16 [16384, 2048], P('expert', 'dp'), may hold values from -6 to 6
- routes: int32 [16384, 2], P('expert'), may hold values from 0 to 127, all different within a row; in each aligned block of 128 rows (0 to 127, 128 to 255, ...) at most 3 rows name the same one
- route_weights: float32 [16384, 2], P('expert'), may hold values from 0.02 to 0.3
- live_tokens: int32 [128], P('expert'), may hold values from 33 to 128, as said below
- gate_codes: bfloat16 [2048, 98304], P('dp', 'expert'), may hold values from -4 to 4
- gate_scales: float32 [16, 768], P('dp', 'expert'), may hold values from 0.011 to 0.044
- up_codes: bfloat16 [2048, 98304], P('dp', 'expert'), may hold values from -4 to 4
- up_scales: float32 [16, 768], P('dp', 'expert'), may hold values from 0.011 to 0.044
- down_codes: bfloat16 [98304, 2048], P('expert', 'dp'), may hold values from -4 to 4
- down_scales: float32 [768, 16], P('expert', 'dp'), may hold values from 0.018 to 0.072
- grad_out: bfloat16 [16384, 2048], P('expert', 'dp'), may hold values from -6 to 6
Outputs:
- grad_tokens: bfloat16 [16384, 2048], P('expert', 'dp')
- grad_route_weights: float32 [16384, 2], P('expert')
- grad_gate_proj: bfloat16 [2048, 98304], P('dp', 'expert')
- grad_up_proj: bfloat16 [2048, 98304], P('dp', 'expert')
- grad_down_proj: bfloat16 [98304, 2048], P('expert', 'dp')
The draws below stay inside these ranges and needn't reach their ends.
Inputs may be any that keep to these rules, and one draw needn't show every extreme that they name: `routes`: in every aligned block of 128 rows (the tokens of one group) each row names 2 different experts, and no expert is named by more than 3 rows of the block; some expert is named by exactly 3 rows of some block. `live_tokens`: some group is full and some group holds the fewest live tokens.
All inputs are finite; a program needn't handle non-finite values.
Results may differ from the reference program's by a relative error of at most 0.023.
Values may be sent and summed in bfloat16 or wider, within the bound.
No kernel may reach another device: no remote copies, remote signals or barrier semaphores. Data moves between devices by JAX's collectives and lax.ppermute only.
A program may use at most 64 MiB of HBM per device.

```python
import math
import jax
import jax.numpy as jnp
import numpy as np
from jax import lax

D = 2048
FF = 768
TOP = 2
BLK = 128
TOK_DEV = 128
GROUPS = 128
EXPERTS = 128
TOKENS = 16384
CAP = 3
N_DP = 4


def draw_live_tokens(key, part):
    first_key, second_key, third_key = jax.random.split(jax.random.fold_in(key, 11), 3)
    lowest = TOK_DEV // 4 + 1
    values = jax.random.randint(first_key, (GROUPS,), lowest, TOK_DEV + 1)
    first = jax.random.randint(second_key, (), 0, GROUPS)
    stride = jax.random.randint(third_key, (), 1, GROUPS)
    second = (first + stride) % GROUPS
    index = jnp.arange(GROUPS)
    values = jnp.where(index == first, TOK_DEV, values)
    values = jnp.where(index == second, lowest, values)
    return values.astype(jnp.int32)


def shard_levels(stream_key, extent, pieces, low, top_value):
    def one(dim, shards_of):
        draws = jax.random.uniform(jax.random.fold_in(jax.random.fold_in(stream_key, 6), dim), (shards_of,), jnp.float32, low / len(pieces), top_value / len(pieces))
        return jnp.repeat(jnp.exp(draws), extent[dim] // shards_of).reshape((-1,) + (1,) * (len(extent) - dim - 1))

    factor_of = one(*pieces[0])
    for cut in pieces[1:]:
        factor_of = factor_of * one(*cut)
    return factor_of


def deal_out(stream_key, own, number, rows, number_of, top, most, skew):
    sequence = jax.random.permutation(stream_key, number_of)
    heavy_load, usual = shares(number_of, rows * top, most, skew, True), shares(number_of, rows * top, most, skew, False)
    places = jnp.arange(number_of)

    def named(lengths, rotation):
        used = int((lengths > 0).sum())
        fixed = max(1, used // 4)
        shifted = fixed + (places - fixed + rotation * (used - fixed)) % max(1, number_of - fixed)
        return jnp.zeros((number_of,), jnp.int32).at[sequence[jnp.where(places < fixed, places, shifted)]].set(jnp.asarray(lengths, jnp.int32))

    lengths = jnp.where(number % 4 == 0, named(heavy_load, number // 4), named(usual, number - number // 4 - 1))
    mixed = jax.random.permutation(jax.random.fold_in(own, 3), number_of)
    donor, taker = mixed[0:number_of // 2 * 2:2], mixed[1:number_of // 2 * 2:2]
    slack = jnp.minimum(lengths[donor] - 1, most - lengths[taker]) // 2
    slack = jnp.where((donor == sequence[0]) | (taker == sequence[0]) | (lengths[taker] == 0), 0, jnp.maximum(slack, 0))
    shifted = jax.random.randint(jax.random.fold_in(own, 4), (number_of // 2,), 0, 1 << 20) % (slack + 1)
    lengths = lengths.at[donor].add(-shifted).at[taker].add(shifted)
    labels = jnp.searchsorted(jnp.cumsum(lengths), jnp.arange(rows * top), side="right").astype(jnp.int32)
    listing = labels.reshape(top, rows).T
    listing = listing[jax.random.permutation(jax.random.fold_in(own, 1), rows)]
    rotation = jax.random.randint(jax.random.fold_in(own, 2), (rows, 1), 0, top)
    return jnp.take_along_axis(listing, (jnp.arange(top)[None, :] + rotation) % top, axis=1)


def shares(count, total, bound, lean, full):
    weights = [(1 << 20) // math.isqrt(standing ** lean) + 1 for standing in range(1, count + 1)]
    largest = bound if full else min(bound, max(-(-total // count), total * weights[0] // sum(weights)))
    least = 1 if total - largest >= count - 1 else 0
    counts, rest = [largest] + [least] * (count - 1), total - largest - least * (count - 1)
    while rest > 0:
        free = [i for i in range(1, count) if counts[i] < largest] or [i for i in range(1, count) if counts[i] < bound]
        whole, budget = sum([weights[i] for i in free]), rest
        for i in free:
            extra = min(bound - counts[i], max(1, budget * weights[i] // whole), rest)
            counts[i] = counts[i] + extra
            rest = rest - extra
    return np.array(counts)


def noise(rng, dims, deviation, most, cuts=(), held_as=jnp.bfloat16):
    loudness = shard_levels(rng, dims, cuts, -0.22, 0.18) if cuts else 1.0
    drawn = jax.random.normal(rng, dims, jnp.float32) * deviation * loudness
    return jnp.minimum(jnp.maximum(drawn, -most), most).astype(held_as)


def setup_inputs(seed: int = 0) -> dict:
    key_of = jax.random.split(jax.random.key(seed), 12)
    tokens = noise(key_of[0], (TOKENS, D), 1.0, 6.0, ((0, 128), (1, 4)))
    routes_keys = jax.random.split(jax.random.fold_in(key_of[1], 1), TOKENS // TOK_DEV)
    routes_turns = jax.random.permutation(jax.random.fold_in(key_of[1], 3), TOKENS // TOK_DEV)
    routes = jax.vmap(lambda own, number: deal_out(jax.random.fold_in(key_of[1], 2), own, number, TOK_DEV, EXPERTS, TOP, CAP, 2))(routes_keys, routes_turns).reshape((TOKENS, TOP))
    route_weights = jnp.clip(0.02 + 0.28 * jax.random.uniform(key_of[2], (TOKENS, TOP), jnp.float32) ** shard_levels(key_of[2], (TOKENS, TOP), ((0, 128),), -0.2, 0.2), 0.02, 0.3)
    live_tokens = draw_live_tokens(jax.random.fold_in(key_of[11], 71), 0)
    gate_codes = noise(key_of[4], (D, EXPERTS * FF), 1.0, 4.0, ((0, 4), (1, 128)))
    gate_scales = jnp.clip(jnp.exp(math.log(0.044) - 1.3862944 * jax.random.uniform(key_of[5], (D // BLK, EXPERTS * FF // BLK), jnp.float32) ** shard_levels(key_of[5], (D // BLK, EXPERTS * FF // BLK), ((0, 4), (1, 128)), -0.2, 0.2)), 0.011, 0.044)
    up_codes = noise(key_of[6], (D, EXPERTS * FF), 1.0, 4.0, ((0, 4), (1, 128)))
    up_scales = jnp.clip(jnp.exp(math.log(0.044) - 1.3862944 * jax.random.uniform(key_of[7], (D // BLK, EXPERTS * FF // BLK), jnp.float32) ** shard_levels(key_of[7], (D // BLK, EXPERTS * FF // BLK), ((0, 4), (1, 128)), -0.2, 0.2)), 0.011, 0.044)
    down_codes = noise(key_of[8], (EXPERTS * FF, D), 1.0, 4.0, ((0, 128), (1, 4)))
    down_scales = jnp.clip(jnp.exp(math.log(0.072) - 1.3862944 * jax.random.uniform(key_of[9], (EXPERTS * FF // BLK, D // BLK), jnp.float32) ** shard_levels(key_of[9], (EXPERTS * FF // BLK, D // BLK), ((0, 128), (1, 4)), -0.2, 0.2)), 0.018, 0.072)
    grad_out = noise(key_of[10], (TOKENS, D), 1.0, 6.0, ((0, 128), (1, 4)))
    return {"tokens": tokens, "routes": routes, "route_weights": route_weights, "live_tokens": live_tokens, "gate_codes": gate_codes, "gate_scales": gate_scales, "up_codes": up_codes, "up_scales": up_scales, "down_codes": down_codes, "down_scales": down_scales, "grad_out": grad_out}


def dequant(codes, scales):
    row_count, col_count = codes.shape
    blocks = codes.astype(jnp.float32).reshape(row_count // BLK, BLK, col_count // BLK, BLK)
    return (blocks * scales[:, None, :, None]).reshape(row_count, col_count).astype(jnp.bfloat16)


def quarter_total(terms):
    rounded = lax.optimization_barrier(terms.astype(jnp.bfloat16))
    return jnp.sum(rounded.astype(jnp.float32), axis=0)


def reference(tokens, routes, route_weights, live_tokens, gate_codes, gate_scales, up_codes, up_scales, down_codes, down_scales, grad_out):
    flat_count = TOK_DEV * TOP
    quarter = D // N_DP
    token_index = jnp.arange(TOKENS, dtype=jnp.int32)
    group_of = token_index // TOK_DEV
    is_live = (token_index % TOK_DEV) < live_tokens[group_of]
    live_flat = jnp.repeat(is_live, TOP).reshape(GROUPS, flat_count)
    expert_ids = routes.reshape(GROUPS, flat_count)
    one_hot = ((expert_ids[:, :, None] == jnp.arange(EXPERTS, dtype=jnp.int32)[None, None, :]) & live_flat[:, :, None]).astype(jnp.int32)
    running = jnp.cumsum(one_hot, axis=1).astype(jnp.int32)
    position = (jnp.sum(one_hot * running, axis=2) - 1).astype(jnp.int32)
    slot_index = jnp.where(live_flat, expert_ids * CAP + position, EXPERTS * CAP).astype(jnp.int32)
    flat_ids = jnp.arange(TOKENS * TOP, dtype=jnp.int32).reshape(GROUPS, flat_count)
    group_rows = jnp.arange(GROUPS, dtype=jnp.int32)[:, None]
    slot_table = jnp.full((GROUPS, EXPERTS * CAP), -1, jnp.int32)
    slot_table = slot_table.at[group_rows, slot_index].set(flat_ids, mode="drop")
    slot_table = slot_table.reshape(GROUPS, EXPERTS, CAP).transpose(1, 0, 2).reshape(EXPERTS, GROUPS * CAP)
    weight_flat = route_weights.reshape(TOKENS * TOP)
    contract_last = (((1,), (1,)), ((), ()))
    contract_first = (((0,), (0,)), ((), ()))

    def per_expert(inputs):
        expert_index, row_ids = inputs
        is_valid = row_ids >= 0
        safe_ids = jnp.maximum(row_ids, 0)
        tok_idx = safe_ids // TOP
        token_rows = jnp.where(is_valid[:, None], tokens[tok_idx], jnp.zeros((), jnp.bfloat16))
        weight_rows = jnp.where(is_valid, weight_flat[safe_ids], jnp.float32(0.0))
        scaled = (weight_rows[:, None] * grad_out[tok_idx].astype(jnp.float32)).astype(jnp.bfloat16)
        col_start = (expert_index * FF).astype(jnp.int32)
        scale_start = (expert_index * (FF // BLK)).astype(jnp.int32)
        w_gate = dequant(lax.dynamic_slice_in_dim(gate_codes, col_start, FF, 1), lax.dynamic_slice_in_dim(gate_scales, scale_start, FF // BLK, 1))
        w_up = dequant(lax.dynamic_slice_in_dim(up_codes, col_start, FF, 1), lax.dynamic_slice_in_dim(up_scales, scale_start, FF // BLK, 1))
        w_down = dequant(lax.dynamic_slice_in_dim(down_codes, col_start, FF, 0), lax.dynamic_slice_in_dim(down_scales, scale_start, FF // BLK, 0))
        row_count = token_rows.shape[0]
        rows_split = token_rows.astype(jnp.float32).reshape(row_count, N_DP, quarter)
        scaled_split = scaled.astype(jnp.float32).reshape(row_count, N_DP, quarter)
        gate_pre = quarter_total(jnp.einsum("rqd,qdf->qrf", rows_split, w_gate.astype(jnp.float32).reshape(N_DP, quarter, FF)))
        up_pre = quarter_total(jnp.einsum("rqd,qdf->qrf", rows_split, w_up.astype(jnp.float32).reshape(N_DP, quarter, FF)))
        grad_hidden = quarter_total(jnp.einsum("rqd,fqd->qrf", scaled_split, w_down.astype(jnp.float32).reshape(FF, N_DP, quarter)))
        sigmoid_gate = jax.nn.sigmoid(gate_pre)
        activated = gate_pre * sigmoid_gate
        hidden = (activated * up_pre).astype(jnp.bfloat16)
        expert_out = jnp.dot(hidden, w_down, preferred_element_type=jnp.float32).astype(jnp.bfloat16)
        gate_delta = (grad_hidden * up_pre * sigmoid_gate * (1.0 + gate_pre * (1.0 - sigmoid_gate))).astype(jnp.bfloat16)
        up_delta = (grad_hidden * activated).astype(jnp.bfloat16)
        grad_part = (lax.dot_general(gate_delta, w_gate, contract_last, preferred_element_type=jnp.float32)
                     + lax.dot_general(up_delta, w_up, contract_last, preferred_element_type=jnp.float32)).astype(jnp.bfloat16)
        grad_gate = lax.dot_general(token_rows, gate_delta, contract_first, preferred_element_type=jnp.float32).astype(jnp.bfloat16)
        grad_up = lax.dot_general(token_rows, up_delta, contract_first, preferred_element_type=jnp.float32).astype(jnp.bfloat16)
        grad_down = lax.dot_general(hidden, scaled, contract_first, preferred_element_type=jnp.float32).astype(jnp.bfloat16)
        return expert_out, grad_part, grad_gate, grad_up, grad_down

    outputs, parts, grad_gate, grad_up, grad_down = lax.map(per_expert, (jnp.arange(EXPERTS, dtype=jnp.int32), slot_table))
    all_ids = slot_table.reshape(EXPERTS * GROUPS * CAP)
    target = jnp.where(all_ids >= 0, all_ids, TOKENS * TOP).astype(jnp.int32)
    out_flat = jnp.zeros((TOKENS * TOP, D), jnp.bfloat16).at[target].set(outputs.reshape(-1, D), mode="drop")
    part_flat = jnp.zeros((TOKENS * TOP, D), jnp.bfloat16).at[target].set(parts.reshape(-1, D), mode="drop")
    expert_out = out_flat.reshape(TOKENS, TOP, D).astype(jnp.float32)
    grad_route_weights = jnp.einsum("td,tkd->tk", grad_out.astype(jnp.float32), expert_out)
    grad_tokens = jnp.sum(part_flat.reshape(TOKENS, TOP, D).astype(jnp.float32), axis=1).astype(jnp.bfloat16)
    grad_gate_proj = grad_gate.transpose(1, 0, 2).reshape(D, EXPERTS * FF)
    grad_up_proj = grad_up.transpose(1, 0, 2).reshape(D, EXPERTS * FF)
    grad_down_proj = grad_down.reshape(EXPERTS * FF, D)
    return grad_tokens, grad_route_weights, grad_gate_proj, grad_up_proj, grad_down_proj
```

```python
import jax
import jax.numpy as jnp
from jax import lax
from jax.experimental import pallas as pl
from jax.experimental.pallas import tpu as pltpu
from jax.sharding import PartitionSpec as P

BF = jnp.bfloat16
F32 = jnp.float32
CAP = 3
QPAD = 16
LAST = (((1,), (1,)), ((), ()))
FIRST = (((0,), (0,)), ((), ()))
VMEM = pl.BlockSpec(memory_space=pltpu.VMEM)
SMEM = pl.BlockSpec(memory_space=pltpu.SMEM)


def split3(v):
    hi = v.astype(BF)
    rest = v - hi.astype(F32)
    mid = rest.astype(BF)
    lo = (rest - mid.astype(F32)).astype(BF)
    return hi, mid, lo


def call(kernel, outs, in_specs, args, flops=0, nbytes=0, scratch=()):
    return pl.pallas_call(
        kernel,
        out_shape=outs,
        in_specs=in_specs,
        out_specs=jax.tree.map(lambda _: VMEM, outs),
        scratch_shapes=scratch,
        cost_estimate=pl.CostEstimate(flops=flops, bytes_accessed=nbytes, transcendentals=0),
    )(*args)


def slot_kernel(live_ref, routes_ref, weights_ref, tokens_ref, grad_ref, send_ref, slots_ref):
    slots, count = slots_ref.shape
    quarter = tokens_ref.shape[1]
    row = lax.broadcasted_iota(jnp.int32, (slots, count), 0)
    token = lax.broadcasted_iota(jnp.int32, (slots, count), 1)
    expert = row // CAP
    live = token < live_ref[0]
    first = (routes_ref[0:1, :] == expert) & live
    second = (routes_ref[1:2, :] == expert) & live
    member = first | second
    before = (
        lax.broadcasted_iota(jnp.int32, (count, count), 0)
        < lax.broadcasted_iota(jnp.int32, (count, count), 1)
    ).astype(BF)
    ahead = jnp.dot(member.astype(BF), before, preferred_element_type=F32)
    chosen = member & (ahead == (row - expert * CAP).astype(F32))
    one_hot = chosen.astype(BF)
    slots_ref[...] = one_hot
    send_ref[:, :quarter] = jnp.dot(
        one_hot, tokens_ref[...], preferred_element_type=F32
    ).astype(BF)
    weight = jnp.where(first, weights_ref[0:1, :], weights_ref[1:2, :])
    weight = jnp.where(chosen, weight, 0.0)
    total = jnp.zeros((slots, quarter), F32)
    for piece in split3(weight):
        total = total + jnp.dot(piece, grad_ref[...], preferred_element_type=F32)
    send_ref[:, quarter:] = total.astype(BF)


def dequant_kernel(gs_ref, us_ref, ds_ref, gc_ref, uc_ref, dc_ref, wg_ref, wu_ref, wd_ref):
    for scale_ref, code_ref, out_ref in (
        (gs_ref, gc_ref, wg_ref),
        (us_ref, uc_ref, wu_ref),
        (ds_ref, dc_ref, wd_ref),
    ):
        for i in range(scale_ref.shape[0]):
            for j in range(scale_ref.shape[1]):
                block = (slice(i * 128, i * 128 + 128), slice(j * 128, j * 128 + 128))
                out_ref[block] = (code_ref[block].astype(F32) * scale_ref[i, j]).astype(BF)


def partial_kernel(rows_ref, wg_ref, wu_ref, wd_ref, out_ref):
    parts = out_ref.shape[0]
    quarter = wg_ref.shape[0]
    span = out_ref.shape[1] // 3
    gate = jnp.dot(rows_ref[:, :quarter], wg_ref[...], preferred_element_type=F32).astype(BF)
    for j in range(parts):
        out_ref[j, 0:span, :] = gate[j * span : (j + 1) * span]
    up = jnp.dot(rows_ref[:, :quarter], wu_ref[...], preferred_element_type=F32).astype(BF)
    for j in range(parts):
        out_ref[j, span : 2 * span, :] = up[j * span : (j + 1) * span]
    back = lax.dot_general(
        rows_ref[:, quarter:], wd_ref[...], LAST, preferred_element_type=F32
    ).astype(BF)
    for j in range(parts):
        out_ref[j, 2 * span : 3 * span, :] = back[j * span : (j + 1) * span]


def act_kernel(part_ref, out_ref):
    parts = part_ref.shape[0]
    span = part_ref.shape[1] // 3

    def total(k):
        lines = slice(k * span, (k + 1) * span)
        acc = part_ref[0, lines, :].astype(F32)
        for j in range(1, parts):
            acc = acc + part_ref[j, lines, :].astype(F32)
        return acc

    gate_pre, up_pre, grad_hidden = total(0), total(1), total(2)
    sig = jax.nn.sigmoid(gate_pre)
    activated = gate_pre * sig
    hidden = (activated * up_pre).astype(BF)
    gate_delta = (grad_hidden * up_pre * sig * (1.0 + gate_pre * (1.0 - sig))).astype(BF)
    up_delta = (grad_hidden * activated).astype(BF)
    prod = hidden.astype(F32) * grad_hidden
    prod = jnp.concatenate([prod, jnp.zeros((128 - span, prod.shape[1]), F32)], axis=0)
    ones = jnp.ones((QPAD, prod.shape[1]), BF)
    score = jnp.zeros((QPAD, 128), F32)
    for piece in split3(prod):
        score = score + lax.dot_general(ones, piece, LAST, preferred_element_type=F32)
    hi, mid, lo = split3(score)
    line = lax.broadcasted_iota(jnp.int32, (QPAD, 128), 0)
    scores = jnp.where(
        line == 0,
        hi.astype(F32),
        jnp.where(line == 1, mid.astype(F32), jnp.where(line == 2, lo.astype(F32), 0.0)),
    ).astype(BF)
    for j in range(parts):
        out_ref[j, 0:span, :] = gate_delta
        out_ref[j, span : 2 * span, :] = up_delta
        out_ref[j, 2 * span : 3 * span, :] = hidden
        out_ref[j, 3 * span : 3 * span + QPAD, 0:128] = scores


def back_kernel(act_ref, wg_ref, wu_ref, out_ref):
    parts = act_ref.shape[0]
    span = (act_ref.shape[1] - QPAD) // 3
    quarter = wg_ref.shape[0]
    eye = (
        lax.broadcasted_iota(jnp.int32, (span, 128), 0)
        == lax.broadcasted_iota(jnp.int32, (span, 128), 1)
    ).astype(BF)
    gate_delta = jnp.concatenate([act_ref[j, 0:span, :] for j in range(parts)], axis=0)
    up_delta = jnp.concatenate([act_ref[j, span : 2 * span, :] for j in range(parts)], axis=0)
    grad = lax.dot_general(gate_delta, wg_ref[...], LAST, preferred_element_type=F32)
    grad = grad + lax.dot_general(up_delta, wu_ref[...], LAST, preferred_element_type=F32)
    out_ref[:, :quarter] = grad.astype(BF)
    for j in range(parts):
        scores = act_ref[j, 3 * span : 3 * span + QPAD, 0:128]
        scores = jnp.concatenate([scores, jnp.zeros((128 - QPAD, 128), BF)], axis=0)
        out_ref[j * span : (j + 1) * span, quarter:] = lax.dot_general(
            eye, scores, LAST, preferred_element_type=F32
        ).astype(BF)


def weight_grad_kernel(rows_ref, act_ref, gg_ref, gu_ref, gd_ref):
    parts = act_ref.shape[0]
    span = (act_ref.shape[1] - QPAD) // 3
    quarter = gg_ref.shape[0]

    def gathered(k):
        return jnp.concatenate(
            [act_ref[j, k * span : (k + 1) * span, :] for j in range(parts)], axis=0
        )

    gg_ref[...] = lax.dot_general(
        rows_ref[:, :quarter], gathered(0), FIRST, preferred_element_type=F32
    ).astype(BF)
    gu_ref[...] = lax.dot_general(
        rows_ref[:, :quarter], gathered(1), FIRST, preferred_element_type=F32
    ).astype(BF)
    gd_ref[...] = lax.dot_general(
        gathered(2), rows_ref[:, quarter:], FIRST, preferred_element_type=F32
    ).astype(BF)


def home_kernel(routes_ref, weights_ref, slots_ref, ret_ref, grad_ref, score_ref):
    slots, count = slots_ref.shape
    quarter = grad_ref.shape[1]
    one_hot = slots_ref[...]
    grad_ref[...] = lax.dot_general(
        one_hot, ret_ref[:, :quarter], FIRST, preferred_element_type=F32
    ).astype(BF)
    pieces = ret_ref[:, quarter:].astype(F32)
    score = pieces[:, 0:1] + pieces[:, 1:2] + pieces[:, 2:3]
    picked = one_hot.astype(F32) * score
    expert = lax.broadcasted_iota(jnp.int32, (slots, count), 0) // CAP
    for k in range(2):
        mine = jnp.where(routes_ref[k : k + 1, :] == expert, picked, 0.0)
        score_ref[k : k + 1, :] = jnp.sum(mine, axis=0, keepdims=True) / weights_ref[k : k + 1, :]


def body(
    tokens,
    routes,
    route_weights,
    live_tokens,
    gate_codes,
    gate_scales,
    up_codes,
    up_scales,
    down_codes,
    down_scales,
    grad_out,
):
    count, quarter = tokens.shape
    hidden_size = gate_codes.shape[1]
    experts = lax.axis_size("expert")
    parts = lax.axis_size("dp")
    slots = experts * CAP
    span = slots // parts
    shape = jax.ShapeDtypeStruct
    routes_t = routes.T
    weights_t = route_weights.T

    send, one_hot = call(
        slot_kernel,
        (shape((slots, 2 * quarter), BF), shape((slots, count), BF)),
        [SMEM, VMEM, VMEM, VMEM, VMEM],
        (live_tokens, routes_t, weights_t, tokens, grad_out),
        flops=2 * slots * count * quarter * 4,
        nbytes=2 * slots * 2 * quarter,
    )
    arrived = lax.all_to_all(
        send.reshape(experts, CAP, 2 * quarter), "expert", split_axis=0, concat_axis=0, tiled=True
    )
    w_gate, w_up, w_down = call(
        dequant_kernel,
        (
            shape(gate_codes.shape, BF),
            shape(up_codes.shape, BF),
            shape(down_codes.shape, BF),
        ),
        [SMEM] * 3 + [VMEM] * 3,
        (gate_scales, up_scales, down_scales, gate_codes, up_codes, down_codes),
        flops=3 * quarter * hidden_size,
        nbytes=12 * quarter * hidden_size,
    )
    rows = arrived.reshape(slots, 2 * quarter)
    part = call(
        partial_kernel,
        shape((parts, 3 * span, hidden_size), BF),
        [VMEM] * 4,
        (rows, w_gate, w_up, w_down),
        flops=6 * slots * quarter * hidden_size,
        nbytes=8 * slots * hidden_size,
    )
    part = lax.all_to_all(part, "dp", split_axis=0, concat_axis=0, tiled=True)
    act = call(
        act_kernel,
        shape((parts, 3 * span + QPAD, hidden_size), BF),
        [VMEM],
        (part,),
        flops=60 * span * hidden_size,
        nbytes=16 * slots * hidden_size,
    )
    act = lax.all_to_all(act, "dp", split_axis=0, concat_axis=0, tiled=True)
    ret = call(
        back_kernel,
        shape((slots, quarter + 128), BF),
        [VMEM] * 3,
        (act, w_gate, w_up),
        flops=4 * slots * quarter * hidden_size,
        nbytes=8 * slots * hidden_size,
    )
    ret = lax.all_to_all(
        ret.reshape(experts, CAP, quarter + 128), "expert", split_axis=0, concat_axis=0, tiled=True
    )
    grad_gate, grad_up, grad_down = call(
        weight_grad_kernel,
        (
            shape((quarter, hidden_size), BF),
            shape((quarter, hidden_size), BF),
            shape((hidden_size, quarter), BF),
        ),
        [VMEM] * 2,
        (rows, act),
        flops=6 * slots * quarter * hidden_size,
        nbytes=16 * slots * hidden_size,
    )
    grad_tokens, grad_weights_t = call(
        home_kernel,
        (shape((count, quarter), BF), shape((2, count), F32)),
        [VMEM] * 4,
        (routes_t, weights_t, one_hot, ret.reshape(slots, quarter + 128)),
        flops=2 * slots * count * quarter,
        nbytes=2 * slots * quarter,
    )
    return (grad_tokens, grad_weights_t.T, grad_gate, grad_up, grad_down)


def solution(mesh):
    placed = (
        P("expert", "dp"),
        P("expert", None),
        P("expert", None),
        P("expert"),
        P("dp", "expert"),
        P("dp", "expert"),
        P("dp", "expert"),
        P("dp", "expert"),
        P("expert", "dp"),
        P("expert", "dp"),
        P("expert", "dp"),
    )
    return jax.shard_map(
        body,
        mesh=mesh,
        in_specs=placed,
        out_specs=(
            P("expert", "dp"),
            P("expert", None),
            P("dp", "expert"),
            P("dp", "expert"),
            P("expert", "dp"),
        ),
        check_vma=False,
    )
```

```python
import jax
import jax.numpy as jnp
from jax import lax
from jax.experimental import pallas as pl
from jax.experimental.pallas import tpu as pltpu
from jax.sharding import PartitionSpec as P

BF = jnp.bfloat16
F32 = jnp.float32
CAP = 3
QPAD = 16
LANES = 128
GRANT = 24 << 20
LAST = (((1,), (1,)), ((), ()))
FIRST = (((0,), (0,)), ((), ()))
VMEM = pl.BlockSpec(memory_space=pltpu.VMEM)
SMEM = pl.BlockSpec(memory_space=pltpu.SMEM)


def split3(v):
    hi = v.astype(BF)
    rest = v - hi.astype(F32)
    mid = rest.astype(BF)
    lo = (rest - mid.astype(F32)).astype(BF)
    return hi, mid, lo


def call(kernel, outs, in_specs, args, flops=0, nbytes=0, scratch=()):
    return pl.pallas_call(
        kernel,
        out_shape=outs,
        in_specs=in_specs,
        out_specs=jax.tree.map(lambda _: VMEM, outs),
        scratch_shapes=scratch,
        compiler_params=pltpu.CompilerParams(vmem_limit_bytes=GRANT),
        cost_estimate=pl.CostEstimate(flops=flops, bytes_accessed=nbytes, transcendentals=0),
    )(*args)


def slot_kernel(live_ref, routes_ref, weights_ref, tokens_ref, grad_ref, send_ref, slots_ref, mix_ref):
    count, quarter = tokens_ref.shape
    experts = slots_ref.shape[0] // CAP
    wide = quarter // LANES
    chunks = 2 * CAP * wide
    expert = lax.broadcasted_iota(jnp.int32, (experts, count), 0)
    live = lax.broadcasted_iota(jnp.int32, (experts, count), 1) < live_ref[0]
    first = (routes_ref[0:1, :] == expert) & live
    second = (routes_ref[1:2, :] == expert) & live
    member = first | second
    before = (
        lax.broadcasted_iota(jnp.int32, (count, count), 0)
        < lax.broadcasted_iota(jnp.int32, (count, count), 1)
    ).astype(BF)
    ahead = jnp.dot(member.astype(BF), before, preferred_element_type=F32)
    weight = jnp.where(first, weights_ref[0:1, :], weights_ref[1:2, :])
    for p in range(CAP):
        chosen = member & (ahead == float(p))
        one_hot = chosen.astype(BF)
        slots_ref[p * experts : (p + 1) * experts, :] = one_hot
        picked = jnp.dot(one_hot, tokens_ref[...], preferred_element_type=F32)
        scaled = jnp.zeros((experts, quarter), F32)
        for piece in split3(jnp.where(chosen, weight, 0.0)):
            scaled = scaled + jnp.dot(piece, grad_ref[...], preferred_element_type=F32)
        for kind, value in enumerate((picked, scaled)):
            for h in range(wide):
                at = (kind * CAP + p) * wide + h
                mix_ref[pl.ds(at, experts, stride=chunks), :] = value[:, h * LANES : (h + 1) * LANES]
    send_ref[...] = mix_ref[...].astype(BF)


def dequant_kernel(gs_ref, us_ref, ds_ref, gc_ref, uc_ref, dc_ref, wg_ref, wu_ref, wd_ref):
    for scale_ref, code_ref, out_ref in (
        (gs_ref, gc_ref, wg_ref),
        (us_ref, uc_ref, wu_ref),
        (ds_ref, dc_ref, wd_ref),
    ):
        for i in range(scale_ref.shape[0]):
            for j in range(scale_ref.shape[1]):
                block = (slice(i * 128, i * 128 + 128), slice(j * 128, j * 128 + 128))
                out_ref[block] = (code_ref[block].astype(F32) * scale_ref[i, j]).astype(BF)


def partial_kernel(got_ref, wg_ref, wu_ref, wd_ref, part_ref, rows_ref, mix_ref):
    parts = part_ref.shape[0]
    quarter = wg_ref.shape[0]
    slots = rows_ref.shape[0]
    span = slots // parts
    groups = slots // CAP
    wide = quarter // LANES
    chunks = 2 * CAP * wide
    mix_ref[...] = got_ref[...].astype(F32)
    for kind in range(2):
        for p in range(CAP):
            for h in range(wide):
                at = (kind * CAP + p) * wide + h
                rows_ref[
                    p * groups : (p + 1) * groups, kind * quarter + h * LANES : kind * quarter + (h + 1) * LANES
                ] = mix_ref[pl.ds(at, groups, stride=chunks), :].astype(BF)
    token_rows = rows_ref[:, :quarter]
    for k, value in enumerate(
        (
            lambda: jnp.dot(token_rows, wg_ref[...], preferred_element_type=F32),
            lambda: jnp.dot(token_rows, wu_ref[...], preferred_element_type=F32),
            lambda: lax.dot_general(rows_ref[:, quarter:], wd_ref[...], LAST, preferred_element_type=F32),
        )
    ):
        result = value().astype(BF)
        for j in range(parts):
            part_ref[j, k * span : (k + 1) * span, :] = result[j * span : (j + 1) * span]


def act_kernel(part_ref, out_ref, hidden_ref):
    parts = part_ref.shape[0]
    span = part_ref.shape[1] // 3

    def total(k):
        lines = slice(k * span, (k + 1) * span)
        acc = part_ref[0, lines, :].astype(F32)
        for j in range(1, parts):
            acc = acc + part_ref[j, lines, :].astype(F32)
        return acc

    gate_pre, up_pre, grad_hidden = total(0), total(1), total(2)
    sig = jax.nn.sigmoid(gate_pre)
    activated = gate_pre * sig
    hidden = (activated * up_pre).astype(BF)
    gate_delta = (grad_hidden * up_pre * sig * (1.0 + gate_pre * (1.0 - sig))).astype(BF)
    up_delta = (grad_hidden * activated).astype(BF)
    prod = hidden.astype(F32) * grad_hidden
    prod = jnp.concatenate([prod, jnp.zeros((128 - span, prod.shape[1]), F32)], axis=0)
    ones = jnp.ones((QPAD, prod.shape[1]), BF)
    score = jnp.zeros((QPAD, 128), F32)
    for piece in split3(prod):
        score = score + lax.dot_general(ones, piece, LAST, preferred_element_type=F32)
    hi, mid, lo = split3(score)
    line = lax.broadcasted_iota(jnp.int32, (QPAD, 128), 0)
    scores = jnp.where(
        line == 0,
        hi.astype(F32),
        jnp.where(line == 1, mid.astype(F32), jnp.where(line == 2, lo.astype(F32), 0.0)),
    ).astype(BF)
    hidden_ref[...] = hidden
    for j in range(parts):
        out_ref[j, 0:span, :] = gate_delta
        out_ref[j, span : 2 * span, :] = up_delta
        out_ref[j, 2 * span : 2 * span + QPAD, 0:128] = scores


def back_kernel(act_ref, wg_ref, wu_ref, out_ref, mix_ref, score_ref):
    parts = act_ref.shape[0]
    span = (act_ref.shape[1] - QPAD) // 2
    quarter = wg_ref.shape[0]
    groups = parts * span // CAP
    wide = quarter // LANES
    chunks = out_ref.shape[0] // groups
    eye = (
        lax.broadcasted_iota(jnp.int32, (span, LANES), 0)
        == lax.broadcasted_iota(jnp.int32, (span, LANES), 1)
    ).astype(BF)
    for j in range(parts):
        scores = act_ref[j, 2 * span : 2 * span + QPAD, 0:LANES]
        scores = jnp.concatenate([scores, jnp.zeros((LANES - QPAD, LANES), BF)], axis=0)
        score_ref[j * span : (j + 1) * span, :] = lax.dot_general(
            eye, scores, LAST, preferred_element_type=F32
        )
    gate_delta = jnp.concatenate([act_ref[j, 0:span, :] for j in range(parts)], axis=0)
    up_delta = jnp.concatenate([act_ref[j, span : 2 * span, :] for j in range(parts)], axis=0)
    grad = lax.dot_general(gate_delta, wg_ref[...], LAST, preferred_element_type=F32)
    grad = grad + lax.dot_general(up_delta, wu_ref[...], LAST, preferred_element_type=F32)
    for p in range(CAP):
        lines = slice(p * groups, (p + 1) * groups)
        for h in range(wide):
            mix_ref[pl.ds(p * wide + h, groups, stride=chunks), :] = grad[lines, h * LANES : (h + 1) * LANES]
        mix_ref[pl.ds(CAP * wide + p, groups, stride=chunks), :] = score_ref[lines, :]
    for c in range(CAP * wide + CAP, chunks):
        mix_ref[pl.ds(c, groups, stride=chunks), :] = jnp.zeros((groups, LANES), F32)
    out_ref[...] = mix_ref[...].astype(BF)


def weight_grad_kernel(me_ref, rows_ref, act_ref, h0_ref, h1_ref, h2_ref, h3_ref, gg_ref, gu_ref, gd_ref):
    parts = act_ref.shape[0]
    span = (act_ref.shape[1] - QPAD) // 2
    quarter = gg_ref.shape[0]

    def gathered(k):
        return jnp.concatenate(
            [act_ref[j, k * span : (k + 1) * span, :] for j in range(parts)], axis=0
        )

    token_rows = rows_ref[:, :quarter]
    gg_ref[...] = lax.dot_general(
        token_rows, gathered(0), FIRST, preferred_element_type=F32
    ).astype(BF)
    gu_ref[...] = lax.dot_general(
        token_rows, gathered(1), FIRST, preferred_element_type=F32
    ).astype(BF)
    hidden, scaled = [], []
    for shift, ref in enumerate((h0_ref, h1_ref, h2_ref, h3_ref)):
        owner = lax.rem(me_ref[0] + parts - shift, parts)
        hidden.append(ref[...])
        scaled.append(rows_ref[pl.ds(pl.multiple_of(owner * span, span), span), quarter:])
    gd_ref[...] = lax.dot_general(
        jnp.concatenate(hidden, axis=0),
        jnp.concatenate(scaled, axis=0),
        FIRST,
        preferred_element_type=F32,
    ).astype(BF)


def home_kernel(routes_ref, weights_ref, slots_ref, ret_ref, grad_ref, score_ref, mix_ref):
    slots, count = slots_ref.shape
    experts = slots // CAP
    quarter = grad_ref.shape[1]
    wide = quarter // LANES
    chunks = ret_ref.shape[0] // experts
    mix_ref[...] = ret_ref[...].astype(F32)

    def chunk(c):
        return mix_ref[pl.ds(c, experts, stride=chunks), :]

    grad = jnp.zeros((count, quarter), F32)
    expert = lax.broadcasted_iota(jnp.int32, (experts, count), 0)
    scores = [jnp.zeros((1, count), F32)] * 2
    for p in range(CAP):
        one_hot = slots_ref[p * experts : (p + 1) * experts, :]
        block = jnp.concatenate([chunk(p * wide + h).astype(BF) for h in range(wide)], axis=1)
        grad = grad + lax.dot_general(one_hot, block, FIRST, preferred_element_type=F32)
        pieces = chunk(CAP * wide + p)
        picked = one_hot.astype(F32) * (pieces[:, 0:1] + pieces[:, 1:2] + pieces[:, 2:3])
        for k in range(2):
            mine = jnp.where(routes_ref[k : k + 1, :] == expert, picked, 0.0)
            scores[k] = scores[k] + jnp.sum(mine, axis=0, keepdims=True)
    grad_ref[...] = grad.astype(BF)
    for k in range(2):
        score_ref[k : k + 1, :] = scores[k] / weights_ref[k : k + 1, :]


def body(
    tokens,
    routes,
    route_weights,
    live_tokens,
    gate_codes,
    gate_scales,
    up_codes,
    up_scales,
    down_codes,
    down_scales,
    grad_out,
):
    count, quarter = tokens.shape
    hidden_size = gate_codes.shape[1]
    experts = lax.axis_size("expert")
    parts = lax.axis_size("dp")
    slots = experts * CAP
    span = slots // parts
    shape = jax.ShapeDtypeStruct
    routes_t = routes.T
    weights_t = route_weights.T

    wide = quarter // LANES
    out_chunks = 2 * CAP * wide
    back_chunks = -(-(CAP * wide + CAP) // 8) * 8
    me = lax.axis_index("dp")

    send, one_hot = call(
        slot_kernel,
        (shape((experts * out_chunks, LANES), BF), shape((slots, count), BF)),
        [SMEM, VMEM, VMEM, VMEM, VMEM],
        (live_tokens, routes_t, weights_t, tokens, grad_out),
        flops=2 * slots * count * quarter * 4,
        nbytes=2 * slots * 2 * quarter,
        scratch=[pltpu.VMEM((experts * out_chunks, LANES), F32)],
    )
    got = lax.all_to_all(
        send.reshape(experts, out_chunks, LANES), "expert", split_axis=0, concat_axis=0, tiled=True
    )
    w_gate, w_up, w_down = call(
        dequant_kernel,
        (
            shape(gate_codes.shape, BF),
            shape(up_codes.shape, BF),
            shape(down_codes.shape, BF),
        ),
        [SMEM] * 3 + [VMEM] * 3,
        (gate_scales, up_scales, down_scales, gate_codes, up_codes, down_codes),
        flops=3 * quarter * hidden_size,
        nbytes=12 * quarter * hidden_size,
    )
    part, rows = call(
        partial_kernel,
        (shape((parts, 3 * span, hidden_size), BF), shape((slots, 2 * quarter), BF)),
        [VMEM] * 4,
        (got.reshape(experts * out_chunks, LANES), w_gate, w_up, w_down),
        flops=6 * slots * quarter * hidden_size,
        nbytes=8 * slots * hidden_size,
        scratch=[pltpu.VMEM((experts * out_chunks, LANES), F32)],
    )
    part = lax.all_to_all(part, "dp", split_axis=0, concat_axis=0, tiled=True)
    act, hidden = call(
        act_kernel,
        (shape((parts, 2 * span + QPAD, hidden_size), BF), shape((span, hidden_size), BF)),
        [VMEM],
        (part,),
        flops=60 * span * hidden_size,
        nbytes=16 * slots * hidden_size,
    )
    act = lax.all_to_all(act, "dp", split_axis=0, concat_axis=0, tiled=True)
    ret = call(
        back_kernel,
        shape((experts * back_chunks, LANES), BF),
        [VMEM] * 3,
        (act, w_gate, w_up),
        flops=4 * slots * quarter * hidden_size,
        nbytes=8 * slots * hidden_size,
        scratch=[
            pltpu.VMEM((experts * back_chunks, LANES), F32),
            pltpu.VMEM((slots, LANES), F32),
        ],
    )
    ret, hidden = lax.optimization_barrier((ret, hidden))
    ret = lax.all_to_all(
        ret.reshape(experts, back_chunks, LANES), "expert", split_axis=0, concat_axis=0, tiled=True
    )
    others = [
        lax.ppermute(hidden, "dp", [(i, (i + shift) % parts) for i in range(parts)])
        for shift in range(1, parts)
    ]
    grad_gate, grad_up, grad_down = call(
        weight_grad_kernel,
        (
            shape((quarter, hidden_size), BF),
            shape((quarter, hidden_size), BF),
            shape((hidden_size, quarter), BF),
        ),
        [SMEM] + [VMEM] * 6,
        (me.reshape(1), rows, act, hidden, *others),
        flops=6 * slots * quarter * hidden_size,
        nbytes=16 * slots * hidden_size,
    )
    grad_tokens, grad_weights_t = call(
        home_kernel,
        (shape((count, quarter), BF), shape((2, count), F32)),
        [VMEM] * 4,
        (routes_t, weights_t, one_hot, ret.reshape(experts * back_chunks, LANES)),
        flops=2 * slots * count * quarter,
        nbytes=2 * slots * quarter,
        scratch=[pltpu.VMEM((experts * back_chunks, LANES), F32)],
    )
    return (grad_tokens, grad_weights_t.T, grad_gate, grad_up, grad_down)


def solution(mesh):
    placed = (
        P("expert", "dp"),
        P("expert", None),
        P("expert", None),
        P("expert"),
        P("dp", "expert"),
        P("dp", "expert"),
        P("dp", "expert"),
        P("dp", "expert"),
        P("expert", "dp"),
        P("expert", "dp"),
        P("expert", "dp"),
    )
    return jax.shard_map(
        body,
        mesh=mesh,
        in_specs=placed,
        out_specs=(
            P("expert", "dp"),
            P("expert", None),
            P("dp", "expert"),
            P("dp", "expert"),
            P("expert", "dp"),
        ),
        check_vma=False,
    )
```

```python
import jax
import jax.numpy as jnp
from jax import lax
from jax.experimental import pallas as pl
from jax.experimental.pallas import tpu as pltpu
from jax.sharding import PartitionSpec as P


BF = jnp.bfloat16
F32 = jnp.float32
CAP = 3
LANES = 128
GRANT = 24 << 20
WIDE = 60 << 20
LAST = (((1,), (1,)), ((), ()))
FIRST = (((0,), (0,)), ((), ()))
VMEM = pl.BlockSpec(memory_space=pltpu.VMEM)
SMEM = pl.BlockSpec(memory_space=pltpu.SMEM)


def split3(v):
    hi = v.astype(BF)
    rest = v - hi.astype(F32)
    mid = rest.astype(BF)
    lo = (rest - mid.astype(F32)).astype(BF)
    return hi, mid, lo


def call(kernel, outs, in_specs, args, flops=0, nbytes=0, scratch=(), grant=GRANT):
    return pl.pallas_call(
        kernel,
        out_shape=outs,
        in_specs=in_specs,
        out_specs=jax.tree.map(lambda _: VMEM, outs),
        scratch_shapes=scratch,
        compiler_params=pltpu.CompilerParams(vmem_limit_bytes=grant),
        cost_estimate=pl.CostEstimate(flops=flops, bytes_accessed=nbytes, transcendentals=0),
    )(*args)


def slot_kernel(live_ref, routes_ref, weights_ref, tokens_ref, grad_ref, send_ref, slots_ref, mix_ref):
    count, quarter = tokens_ref.shape
    experts = slots_ref.shape[0] // CAP
    wide = quarter // LANES
    chunks = 2 * CAP * wide
    expert = lax.broadcasted_iota(jnp.int32, (experts, count), 0)
    live = lax.broadcasted_iota(jnp.int32, (experts, count), 1) < live_ref[0]
    first = (routes_ref[0:1, :] == expert) & live
    second = (routes_ref[1:2, :] == expert) & live
    member = first | second
    before = (
        lax.broadcasted_iota(jnp.int32, (count, count), 0)
        < lax.broadcasted_iota(jnp.int32, (count, count), 1)
    ).astype(BF)
    ahead = jnp.dot(member.astype(BF), before, preferred_element_type=F32)
    weight = jnp.where(first, weights_ref[0:1, :], weights_ref[1:2, :])
    for p in range(CAP):
        chosen = member & (ahead == float(p))
        one_hot = chosen.astype(BF)
        slots_ref[p * experts : (p + 1) * experts, :] = one_hot
        picked = jnp.dot(one_hot, tokens_ref[...], preferred_element_type=F32)
        scaled = jnp.zeros((experts, quarter), F32)
        for piece in split3(jnp.where(chosen, weight, 0.0)):
            scaled = scaled + jnp.dot(piece, grad_ref[...], preferred_element_type=F32)
        for kind, value in enumerate((picked, scaled)):
            for h in range(wide):
                at = (kind * CAP + p) * wide + h
                mix_ref[pl.ds(at, experts, stride=chunks), :] = value[:, h * LANES : (h + 1) * LANES]
    send_ref[...] = mix_ref[...].astype(BF)


def dequant(scale_ref, code_ref, out_ref, base):
    for i in range(scale_ref.shape[0]):
        for j in range(scale_ref.shape[1]):
            lines = slice(i * LANES, (i + 1) * LANES)
            lanes = slice(j * LANES, (j + 1) * LANES)
            out_ref[base + i * LANES : base + (i + 1) * LANES, lanes] = (
                code_ref[lines, lanes].astype(F32) * scale_ref[i, j]
            ).astype(BF)


def dequant_pair_kernel(gs_ref, us_ref, gc_ref, uc_ref, out_ref):
    dequant(gs_ref, gc_ref, out_ref, 0)
    dequant(us_ref, uc_ref, out_ref, gc_ref.shape[0])


def dequant_one_kernel(ds_ref, dc_ref, out_ref):
    dequant(ds_ref, dc_ref, out_ref, 0)


def row_kernel(got_ref, wd_ref, out_ref, rows_ref, mix_ref):
    parts, span, _ = out_ref.shape
    quarter = rows_ref.shape[1] // 2
    groups = rows_ref.shape[0] // CAP
    wide = quarter // LANES
    chunks = 2 * CAP * wide
    mix_ref[...] = got_ref[...].astype(F32)
    for kind in range(2):
        for p in range(CAP):
            for h in range(wide):
                at = (kind * CAP + p) * wide + h
                lane = kind * quarter + h * LANES
                rows_ref[p * groups : (p + 1) * groups, lane : lane + LANES] = mix_ref[
                    pl.ds(at, groups, stride=chunks), :
                ].astype(BF)
    back = lax.dot_general(
        rows_ref[:, quarter:], wd_ref[...], LAST, preferred_element_type=F32
    ).astype(BF)
    for j in range(parts):
        lines = slice(j * span, (j + 1) * span)
        out_ref[j, :, :quarter] = rows_ref[lines, :quarter]
        out_ref[j, :, quarter:] = back[lines]


def act_kernel(me_ref, part_ref, own_ref, next_ref, far_ref, prev_ref, out_ref, act_ref):
    parts, span, _ = part_ref.shape
    quarter = own_ref.shape[0] // 2
    owners = [lax.rem(me_ref[0] + shift, parts) for shift in range(parts)]

    blocks = (own_ref, next_ref, far_ref, prev_ref)

    def gate_of(shift):
        return blocks[shift][:quarter, :]

    def up_of(shift):
        return blocks[shift][quarter:, :]

    gate_pre = up_pre = 0.0
    for shift in range(parts):
        token_rows = part_ref[owners[shift], :, :quarter]
        gate = jnp.dot(token_rows, gate_of(shift), preferred_element_type=F32)
        gate_pre = gate_pre + gate.astype(BF).astype(F32)
        up = jnp.dot(token_rows, up_of(shift), preferred_element_type=F32)
        up_pre = up_pre + up.astype(BF).astype(F32)
    grad_hidden = part_ref[0, :, quarter:].astype(F32)
    for j in range(1, parts):
        grad_hidden = grad_hidden + part_ref[j, :, quarter:].astype(F32)
    sig = jax.nn.sigmoid(gate_pre)
    activated = gate_pre * sig
    hidden = (activated * up_pre).astype(BF)
    gate_delta = (grad_hidden * up_pre * sig * (1.0 + gate_pre * (1.0 - sig))).astype(BF)
    up_delta = (grad_hidden * activated).astype(BF)
    act_ref[0:span, :] = gate_delta
    act_ref[span : 2 * span, :] = up_delta
    act_ref[2 * span : 3 * span, :] = hidden
    score = jnp.sum(hidden.astype(F32) * grad_hidden, axis=1, keepdims=True)
    lane = lax.broadcasted_iota(jnp.int32, (span, LANES), 1)
    hi, mid, lo = (v.astype(F32) for v in split3(score))
    scores = jnp.where(
        lane == 0, hi, jnp.where(lane == 1, mid, jnp.where(lane == 2, lo, 0.0))
    ).astype(BF)
    for shift in range(parts):
        grad = lax.dot_general(gate_delta, gate_of(shift), LAST, preferred_element_type=F32)
        grad = grad + lax.dot_general(up_delta, up_of(shift), LAST, preferred_element_type=F32)
        out_ref[owners[shift], :, :quarter] = grad.astype(BF)
        out_ref[owners[shift], :, quarter:] = scores


def pack_kernel(grad_ref, out_ref, mix_ref):
    groups = grad_ref.shape[0] // CAP
    wide = grad_ref.shape[1] // LANES - 1
    chunks = out_ref.shape[0] // groups
    for p in range(CAP):
        for h in range(wide + 1):
            at = p * wide + h if h < wide else CAP * wide + p
            mix_ref[pl.ds(at, groups, stride=chunks), :] = grad_ref[
                p * groups : (p + 1) * groups, h * LANES : (h + 1) * LANES
            ].astype(F32)
    for c in range(CAP * wide + CAP, chunks):
        mix_ref[pl.ds(c, groups, stride=chunks), :] = jnp.zeros((groups, LANES), F32)
    out_ref[...] = mix_ref[...].astype(BF)


def weight_grad_kernel(me_ref, rows_ref, a0_ref, a1_ref, a2_ref, a3_ref, gg_ref, gu_ref, gd_ref):
    parts = 4
    span = a0_ref.shape[0] // 3
    quarter = gg_ref.shape[0]
    rows, acts = [], []
    for shift, ref in enumerate((a0_ref, a1_ref, a2_ref, a3_ref)):
        owner = lax.rem(me_ref[0] + parts - shift, parts)
        rows.append(rows_ref[pl.ds(pl.multiple_of(owner * span, span), span), :])
        acts.append(ref)
    rows = jnp.concatenate(rows, axis=0)

    def gathered(k):
        return jnp.concatenate([ref[k * span : (k + 1) * span, :] for ref in acts], axis=0)

    token_rows = rows[:, :quarter]
    gg_ref[...] = lax.dot_general(
        token_rows, gathered(0), FIRST, preferred_element_type=F32
    ).astype(BF)
    gu_ref[...] = lax.dot_general(
        token_rows, gathered(1), FIRST, preferred_element_type=F32
    ).astype(BF)
    gd_ref[...] = lax.dot_general(
        gathered(2), rows[:, quarter:], FIRST, preferred_element_type=F32
    ).astype(BF)


def home_kernel(routes_ref, weights_ref, slots_ref, ret_ref, grad_ref, score_ref, mix_ref):
    slots, count = slots_ref.shape
    experts = slots // CAP
    quarter = grad_ref.shape[1]
    wide = quarter // LANES
    chunks = ret_ref.shape[0] // experts
    mix_ref[...] = ret_ref[...].astype(F32)

    def chunk(c):
        return mix_ref[pl.ds(c, experts, stride=chunks), :]

    grad = jnp.zeros((count, quarter), F32)
    expert = lax.broadcasted_iota(jnp.int32, (experts, count), 0)
    scores = [jnp.zeros((1, count), F32)] * 2
    for p in range(CAP):
        one_hot = slots_ref[p * experts : (p + 1) * experts, :]
        block = jnp.concatenate([chunk(p * wide + h).astype(BF) for h in range(wide)], axis=1)
        grad = grad + lax.dot_general(one_hot, block, FIRST, preferred_element_type=F32)
        pieces = chunk(CAP * wide + p)
        picked = one_hot.astype(F32) * (pieces[:, 0:1] + pieces[:, 1:2] + pieces[:, 2:3])
        for k in range(2):
            mine = jnp.where(routes_ref[k : k + 1, :] == expert, picked, 0.0)
            scores[k] = scores[k] + jnp.sum(mine, axis=0, keepdims=True)
    grad_ref[...] = grad.astype(BF)
    for k in range(2):
        score_ref[k : k + 1, :] = scores[k] / weights_ref[k : k + 1, :]


def layer(
    tokens,
    routes,
    route_weights,
    live_tokens,
    gate_codes,
    gate_scales,
    up_codes,
    up_scales,
    down_codes,
    down_scales,
    grad_out,
):
    count, quarter = tokens.shape
    hidden_size = gate_codes.shape[1]
    experts = lax.axis_size("expert")
    parts = lax.axis_size("dp")
    slots = experts * CAP
    span = slots // parts
    shape = jax.ShapeDtypeStruct
    routes_t = routes.T
    weights_t = route_weights.T

    wide = quarter // LANES
    out_chunks = 2 * CAP * wide
    back_chunks = -(-(CAP * wide + CAP) // 8) * 8
    me = lax.axis_index("dp")

    def turn(value, shift):
        return lax.ppermute(value, "dp", [(i, (i + shift) % parts) for i in range(parts)])

    w_own = call(
        dequant_pair_kernel,
        shape((2 * quarter, hidden_size), BF),
        [SMEM] * 2 + [VMEM] * 2,
        (gate_scales, up_scales, gate_codes, up_codes),
        grant=WIDE,
        flops=2 * quarter * hidden_size,
        nbytes=8 * quarter * hidden_size,
    )
    w_prev = turn(w_own, 1)
    send, one_hot = call(
        slot_kernel,
        (shape((experts * out_chunks, LANES), BF), shape((slots, count), BF)),
        [SMEM, VMEM, VMEM, VMEM, VMEM],
        (live_tokens, routes_t, weights_t, tokens, grad_out),
        flops=2 * slots * count * quarter * 4,
        nbytes=2 * slots * 2 * quarter,
        scratch=[pltpu.VMEM((experts * out_chunks, LANES), F32)],
    )
    got = lax.all_to_all(
        send.reshape(experts, out_chunks, LANES), "expert", split_axis=0, concat_axis=0, tiled=True
    )
    w_next = turn(w_own, -1)
    w_far = turn(w_prev, 1)
    w_down = call(
        dequant_one_kernel,
        shape(down_codes.shape, BF),
        [SMEM, VMEM],
        (down_scales, down_codes),
        flops=quarter * hidden_size,
        nbytes=4 * quarter * hidden_size,
    )
    part, rows = call(
        row_kernel,
        (shape((parts, span, quarter + hidden_size), BF), shape((slots, 2 * quarter), BF)),
        [VMEM] * 2,
        (got.reshape(experts * out_chunks, LANES), w_down),
        flops=2 * slots * quarter * hidden_size,
        nbytes=8 * slots * hidden_size,
        scratch=[pltpu.VMEM((experts * out_chunks, LANES), F32)],
    )
    part = lax.all_to_all(part, "dp", split_axis=0, concat_axis=0, tiled=True)
    grad, acts = call(
        act_kernel,
        (shape((parts, span, quarter + LANES), BF), shape((3 * span, hidden_size), BF)),
        [SMEM] + [VMEM] * 5,
        (me.reshape(1), part, w_own, w_next, w_far, w_prev),
        flops=8 * slots * quarter * hidden_size,
        nbytes=16 * quarter * hidden_size,
    )
    grad = lax.all_to_all(grad, "dp", split_axis=0, concat_axis=0, tiled=True)
    ret = call(
        pack_kernel,
        shape((experts * back_chunks, LANES), BF),
        [VMEM],
        (grad.reshape(slots, quarter + LANES),),
        nbytes=8 * slots * quarter,
        scratch=[pltpu.VMEM((experts * back_chunks, LANES), F32)],
    )
    ret, acts = lax.optimization_barrier((ret, acts))
    ret = lax.all_to_all(
        ret.reshape(experts, back_chunks, LANES), "expert", split_axis=0, concat_axis=0, tiled=True
    )
    grad_gate, grad_up, grad_down = call(
        weight_grad_kernel,
        (
            shape((quarter, hidden_size), BF),
            shape((quarter, hidden_size), BF),
            shape((hidden_size, quarter), BF),
        ),
        [SMEM] + [VMEM] * 5,
        (me.reshape(1), rows, acts, turn(acts, 1), turn(acts, 2), turn(acts, 3)),
        flops=6 * slots * quarter * hidden_size,
        nbytes=16 * slots * hidden_size,
    )
    grad_tokens, grad_weights_t = call(
        home_kernel,
        (shape((count, quarter), BF), shape((2, count), F32)),
        [VMEM] * 4,
        (routes_t, weights_t, one_hot, ret.reshape(experts * back_chunks, LANES)),
        flops=2 * slots * count * quarter,
        nbytes=2 * slots * quarter,
        scratch=[pltpu.VMEM((experts * back_chunks, LANES), F32)],
    )
    return (grad_tokens, grad_weights_t.T, grad_gate, grad_up, grad_down)


def solution(mesh):
    placed = (
        P("expert", "dp"),
        P("expert", None),
        P("expert", None),
        P("expert"),
        P("dp", "expert"),
        P("dp", "expert"),
        P("dp", "expert"),
        P("dp", "expert"),
        P("expert", "dp"),
        P("expert", "dp"),
        P("expert", "dp"),
    )
    return jax.shard_map(
        layer,
        mesh=mesh,
        in_specs=placed,
        out_specs=(
            P("expert", "dp"),
            P("expert", None),
            P("dp", "expert"),
            P("dp", "expert"),
            P("expert", "dp"),
        ),
        check_vma=False,
    )
```

```python
import jax
import jax.numpy as jnp
from jax import lax
from jax.experimental import pallas as pl
from jax.experimental.pallas import tpu as pltpu
from jax.sharding import PartitionSpec as P


BF = jnp.bfloat16
F32 = jnp.float32
CAP = 3
LANES = 128
GRANT = 62 << 20
MIDDLE = 50 << 20
SMALL = 24 << 20
LAST = (((1,), (1,)), ((), ()))
FIRST = (((0,), (0,)), ((), ()))
VMEM = pl.BlockSpec(memory_space=pltpu.VMEM)
SMEM = pl.BlockSpec(memory_space=pltpu.SMEM)
ANY = pl.BlockSpec(memory_space=pl.ANY)


def split3(v):
    hi = v.astype(BF)
    rest = v - hi.astype(F32)
    mid = rest.astype(BF)
    lo = (rest - mid.astype(F32)).astype(BF)
    return hi, mid, lo


def call(kernel, outs, in_specs, args, flops=0, nbytes=0, scratch=(), grant=GRANT, place=VMEM):
    return pl.pallas_call(
        kernel,
        out_shape=outs,
        in_specs=in_specs,
        out_specs=jax.tree.map(lambda _: place, outs),
        scratch_shapes=scratch,
        compiler_params=pltpu.CompilerParams(vmem_limit_bytes=grant),
        cost_estimate=pl.CostEstimate(flops=flops, bytes_accessed=nbytes, transcendentals=0),
    )(*args)


def slot_kernel(live_ref, routes_ref, weights_ref, tokens_ref, grad_ref, send_ref, slots_ref, mix_ref):
    count, quarter = tokens_ref.shape
    experts = slots_ref.shape[0] // CAP
    wide = quarter // LANES
    chunks = 2 * CAP * wide
    expert = lax.broadcasted_iota(jnp.int32, (experts, count), 0)
    live = lax.broadcasted_iota(jnp.int32, (experts, count), 1) < live_ref[0]
    first = (routes_ref[0:1, :] == expert) & live
    second = (routes_ref[1:2, :] == expert) & live
    member = first | second
    before = (
        lax.broadcasted_iota(jnp.int32, (count, count), 0)
        < lax.broadcasted_iota(jnp.int32, (count, count), 1)
    ).astype(BF)
    ahead = jnp.dot(member.astype(BF), before, preferred_element_type=F32)
    weight = jnp.where(first, weights_ref[0:1, :], weights_ref[1:2, :])
    for p in range(CAP):
        chosen = member & (ahead == float(p))
        one_hot = chosen.astype(BF)
        slots_ref[p * experts : (p + 1) * experts, :] = one_hot
        picked = jnp.dot(one_hot, tokens_ref[...], preferred_element_type=F32)
        scaled = jnp.zeros((experts, quarter), F32)
        for piece in split3(jnp.where(chosen, weight, 0.0)):
            scaled = scaled + jnp.dot(piece, grad_ref[...], preferred_element_type=F32)
        for kind, value in enumerate((picked, scaled)):
            for h in range(wide):
                at = (kind * CAP + p) * wide + h
                mix_ref[pl.ds(at, experts, stride=chunks), :] = value[:, h * LANES : (h + 1) * LANES]
    send_ref[...] = mix_ref[...].astype(BF)


def dequant(scale_ref, code_ref, out_ref, base):
    for i in range(scale_ref.shape[0]):
        for j in range(scale_ref.shape[1]):
            lines = slice(i * LANES, (i + 1) * LANES)
            lanes = slice(j * LANES, (j + 1) * LANES)
            out_ref[base + i * LANES : base + (i + 1) * LANES, lanes] = (
                code_ref[lines, lanes].astype(F32) * scale_ref[i, j]
            ).astype(BF)


def dequant_pair_kernel(gs_ref, us_ref, gc_ref, uc_ref, out_ref):
    dequant(gs_ref, gc_ref, out_ref, 0)
    dequant(us_ref, uc_ref, out_ref, gc_ref.shape[0])


def dequant_one_kernel(ds_ref, dc_ref, out_ref):
    dequant(ds_ref, dc_ref, out_ref, 0)


def row_kernel(got_hbm, wd_hbm, out_hbm, rows_hbm, got_ref, wd_ref, out_ref, rows_ref, mix_ref, sems):
    parts, span, _ = out_ref.shape
    quarter = rows_ref.shape[1] // 2
    groups = rows_ref.shape[0] // CAP
    near = groups // parts
    wide = quarter // LANES
    chunks = 2 * CAP * wide
    load = [
        pltpu.make_async_copy(got_hbm, got_ref, sems.at[0]),
        pltpu.make_async_copy(wd_hbm, wd_ref, sems.at[1]),
    ]
    for copy in load:
        copy.start()
    load[0].wait()
    mix_ref[...] = got_ref[...].astype(F32)
    for kind in range(2):
        for p in range(CAP):
            for h in range(wide):
                at = (kind * CAP + p) * wide + h
                lane = kind * quarter + h * LANES
                value = mix_ref[pl.ds(at, groups, stride=chunks), :].astype(BF)
                for j in range(parts):
                    line = j * span + p * near
                    piece = value[j * near : (j + 1) * near]
                    rows_ref[line : line + near, lane : lane + LANES] = piece
                    if kind == 0:
                        out_ref[j, p * near : (p + 1) * near, lane : lane + LANES] = piece
    save = [pltpu.make_async_copy(rows_ref, rows_hbm, sems.at[2])]
    save[0].start()
    load[1].wait()
    back = lax.dot_general(
        rows_ref[:, quarter:], wd_ref[...], LAST, preferred_element_type=F32
    ).astype(BF)
    for j in range(parts):
        out_ref[j, :, quarter:] = back[j * span : (j + 1) * span]
        copy = pltpu.make_async_copy(out_ref.at[j], out_hbm.at[j], sems.at[3 + j])
        copy.start()
        save.append(copy)
    for copy in save:
        copy.wait()


def act_kernel(
    me_ref, part_ref, own_hbm, next_hbm, far_gate_hbm, far_up_hbm, prev_hbm, out_ref, act_ref, w_ref, mix_ref, sems
):
    parts, span, _ = part_ref.shape
    near = span // CAP
    quarter = w_ref.shape[1] // 2
    wide = quarter // LANES
    chunks = out_ref.shape[1] // near
    owners = [lax.rem(me_ref[0] + shift, parts) for shift in range(parts)]
    copies = [
        pltpu.make_async_copy(source, target, sems.at[n])
        for n, (source, target) in enumerate(
            (
                (own_hbm, w_ref.at[0]),
                (next_hbm, w_ref.at[1]),
                (prev_hbm, w_ref.at[3]),
                (far_gate_hbm, w_ref.at[2, :quarter]),
                (far_up_hbm, w_ref.at[2, quarter:]),
            )
        )
    ]
    for copy in copies:
        copy.start()
    grad_hidden = part_ref[0, :, quarter:].astype(F32)
    for j in range(1, parts):
        grad_hidden = grad_hidden + part_ref[j, :, quarter:].astype(F32)
    gate_pre = up_pre = 0.0
    for shift, needed in ((0, (0,)), (1, (1,)), (3, (2,)), (2, (3, 4))):
        for n in needed:
            copies[n].wait()
        token_rows = part_ref[owners[shift], :, :quarter]
        gate = jnp.dot(token_rows, w_ref[shift, :quarter, :], preferred_element_type=F32)
        gate_pre = gate_pre + gate.astype(BF).astype(F32)
        up = jnp.dot(token_rows, w_ref[shift, quarter:, :], preferred_element_type=F32)
        up_pre = up_pre + up.astype(BF).astype(F32)
    sig = jax.nn.sigmoid(gate_pre)
    activated = gate_pre * sig
    hidden = (activated * up_pre).astype(BF)
    gate_delta = (grad_hidden * up_pre * sig * (1.0 + gate_pre * (1.0 - sig))).astype(BF)
    up_delta = (grad_hidden * activated).astype(BF)
    act_ref[0:span, :] = gate_delta
    act_ref[span : 2 * span, :] = up_delta
    act_ref[2 * span : 3 * span, :] = hidden
    score = jnp.sum(hidden.astype(F32) * grad_hidden, axis=1, keepdims=True)
    lane = lax.broadcasted_iota(jnp.int32, (span, LANES), 1)
    hi, mid, lo = (v.astype(F32) for v in split3(score))
    scores = jnp.where(lane == 0, hi, jnp.where(lane == 1, mid, jnp.where(lane == 2, lo, 0.0)))
    for p in range(CAP):
        mix_ref[pl.ds(CAP * wide + p, near, stride=chunks), :] = scores[p * near : (p + 1) * near]
    for c in range(CAP * wide + CAP, chunks):
        mix_ref[pl.ds(c, near, stride=chunks), :] = jnp.zeros((near, LANES), F32)
    for shift in range(parts):
        grad = lax.dot_general(
            gate_delta, w_ref[shift, :quarter, :], LAST, preferred_element_type=F32
        )
        grad = grad + lax.dot_general(
            up_delta, w_ref[shift, quarter:, :], LAST, preferred_element_type=F32
        )
        for p in range(CAP):
            for h in range(wide):
                mix_ref[pl.ds(p * wide + h, near, stride=chunks), :] = grad[
                    p * near : (p + 1) * near, h * LANES : (h + 1) * LANES
                ]
        out_ref[owners[shift]] = mix_ref[...].astype(BF)


def weight_grad_kernel(me_ref, rows_ref, a0_ref, a1_ref, a2_ref, a3_ref, gg_ref, gu_ref, gd_ref):
    parts = 4
    span = a0_ref.shape[0] // 3
    quarter = gg_ref.shape[0]
    rows, acts = [], []
    for shift, ref in enumerate((a0_ref, a1_ref, a2_ref, a3_ref)):
        owner = lax.rem(me_ref[0] + parts - shift, parts)
        rows.append(rows_ref[pl.ds(pl.multiple_of(owner * span, span), span), :])
        acts.append(ref)
    rows = jnp.concatenate(rows, axis=0)

    def gathered(k):
        return jnp.concatenate([ref[k * span : (k + 1) * span, :] for ref in acts], axis=0)

    token_rows = rows[:, :quarter]
    gg_ref[...] = lax.dot_general(
        token_rows, gathered(0), FIRST, preferred_element_type=F32
    ).astype(BF)
    gu_ref[...] = lax.dot_general(
        token_rows, gathered(1), FIRST, preferred_element_type=F32
    ).astype(BF)
    gd_ref[...] = lax.dot_general(
        gathered(2), rows[:, quarter:], FIRST, preferred_element_type=F32
    ).astype(BF)


def home_kernel(routes_ref, weights_ref, slots_ref, ret_ref, grad_ref, score_ref, mix_ref):
    slots, count = slots_ref.shape
    experts = slots // CAP
    quarter = grad_ref.shape[1]
    wide = quarter // LANES
    chunks = ret_ref.shape[0] // experts
    mix_ref[...] = ret_ref[...].astype(F32)

    def chunk(c):
        return mix_ref[pl.ds(c, experts, stride=chunks), :]

    grad = jnp.zeros((count, quarter), F32)
    expert = lax.broadcasted_iota(jnp.int32, (experts, count), 0)
    scores = [jnp.zeros((1, count), F32)] * 2
    for p in range(CAP):
        one_hot = slots_ref[p * experts : (p + 1) * experts, :]
        block = jnp.concatenate([chunk(p * wide + h).astype(BF) for h in range(wide)], axis=1)
        grad = grad + lax.dot_general(one_hot, block, FIRST, preferred_element_type=F32)
        pieces = chunk(CAP * wide + p)
        picked = one_hot.astype(F32) * (pieces[:, 0:1] + pieces[:, 1:2] + pieces[:, 2:3])
        for k in range(2):
            mine = jnp.where(routes_ref[k : k + 1, :] == expert, picked, 0.0)
            scores[k] = scores[k] + jnp.sum(mine, axis=0, keepdims=True)
    grad_ref[...] = grad.astype(BF)
    for k in range(2):
        score_ref[k : k + 1, :] = scores[k] / weights_ref[k : k + 1, :]


def layer(
    tokens,
    routes,
    route_weights,
    live_tokens,
    gate_codes,
    gate_scales,
    up_codes,
    up_scales,
    down_codes,
    down_scales,
    grad_out,
):
    count, quarter = tokens.shape
    hidden_size = gate_codes.shape[1]
    experts = lax.axis_size("expert")
    parts = lax.axis_size("dp")
    slots = experts * CAP
    span = slots // parts
    shape = jax.ShapeDtypeStruct
    routes_t = routes.T
    weights_t = route_weights.T

    wide = quarter // LANES
    out_chunks = 2 * CAP * wide
    back_chunks = -(-(CAP * wide + CAP) // 8) * 8
    me = lax.axis_index("dp")

    def turn(value, shift):
        return lax.ppermute(value, "dp", [(i, (i + shift) % parts) for i in range(parts)])

    w_own = call(
        dequant_pair_kernel,
        shape((2 * quarter, hidden_size), BF),
        [SMEM] * 2 + [VMEM] * 2,
        (gate_scales, up_scales, gate_codes, up_codes),
        flops=2 * quarter * hidden_size,
        nbytes=8 * quarter * hidden_size,
    )
    w_prev = turn(w_own, 1)
    w_next = turn(w_own, -1)
    send, one_hot = call(
        slot_kernel,
        (shape((experts * out_chunks, LANES), BF), shape((slots, count), BF)),
        [SMEM, VMEM, VMEM, VMEM, VMEM],
        (live_tokens, routes_t, weights_t, tokens, grad_out),
        flops=2 * slots * count * quarter * 4,
        nbytes=2 * slots * 2 * quarter,
        scratch=[pltpu.VMEM((experts * out_chunks, LANES), F32)],
    )
    got = lax.all_to_all(
        send.reshape(experts, out_chunks, LANES), "expert", split_axis=0, concat_axis=0, tiled=True
    )
    far_gate = turn(w_next[:quarter], -1)
    far_up = turn(w_prev[quarter:], 1)
    w_down = call(
        dequant_one_kernel,
        shape(down_codes.shape, BF),
        [SMEM, VMEM],
        (down_scales, down_codes),
        flops=quarter * hidden_size,
        nbytes=4 * quarter * hidden_size,
    )
    part, rows = call(
        row_kernel,
        (shape((parts, span, quarter + hidden_size), BF), shape((slots, 2 * quarter), BF)),
        [ANY] * 2,
        (got.reshape(experts * out_chunks, LANES), w_down),
        flops=2 * slots * quarter * hidden_size,
        nbytes=8 * slots * hidden_size,
        scratch=[
            pltpu.VMEM((experts * out_chunks, LANES), BF),
            pltpu.VMEM((hidden_size, quarter), BF),
            pltpu.VMEM((parts, span, quarter + hidden_size), BF),
            pltpu.VMEM((slots, 2 * quarter), BF),
            pltpu.VMEM((experts * out_chunks, LANES), F32),
            pltpu.SemaphoreType.DMA((3 + parts,)),
        ],
        place=ANY,
    )
    part = lax.all_to_all(part, "dp", split_axis=0, concat_axis=0, tiled=True)
    ret, acts = call(
        act_kernel,
        (
            shape((parts, span // CAP * back_chunks, LANES), BF),
            shape((3 * span, hidden_size), BF),
        ),
        [SMEM, VMEM] + [ANY] * 5,
        (me.reshape(1), part, w_own, w_next, far_gate, far_up, w_prev),
        grant=MIDDLE,
        flops=8 * slots * quarter * hidden_size,
        nbytes=16 * quarter * hidden_size,
        scratch=[
            pltpu.VMEM((parts, 2 * quarter, hidden_size), BF),
            pltpu.VMEM((span // CAP * back_chunks, LANES), F32),
            pltpu.SemaphoreType.DMA((5,)),
        ],
    )
    ret = lax.all_to_all(ret, "dp", split_axis=0, concat_axis=0, tiled=True)
    ret, acts = lax.optimization_barrier((ret, acts))
    ret = lax.all_to_all(
        ret.reshape(experts, back_chunks, LANES), "expert", split_axis=0, concat_axis=0, tiled=True
    )
    grad_gate, grad_up, grad_down = call(
        weight_grad_kernel,
        (
            shape((quarter, hidden_size), BF),
            shape((quarter, hidden_size), BF),
            shape((hidden_size, quarter), BF),
        ),
        [SMEM] + [VMEM] * 5,
        (me.reshape(1), rows, acts, turn(acts, 1), turn(acts, 2), turn(acts, 3)),
        grant=SMALL,
        flops=6 * slots * quarter * hidden_size,
        nbytes=16 * slots * hidden_size,
    )
    grad_tokens, grad_weights_t = call(
        home_kernel,
        (shape((count, quarter), BF), shape((2, count), F32)),
        [VMEM] * 4,
        (routes_t, weights_t, one_hot, ret.reshape(experts * back_chunks, LANES)),
        grant=SMALL,
        flops=2 * slots * count * quarter,
        nbytes=2 * slots * quarter,
        scratch=[pltpu.VMEM((experts * back_chunks, LANES), F32)],
    )
    return (grad_tokens, grad_weights_t.T, grad_gate, grad_up, grad_down)


def solution(mesh):
    placed = (
        P("expert", "dp"),
        P("expert", None),
        P("expert", None),
        P("expert"),
        P("dp", "expert"),
        P("dp", "expert"),
        P("dp", "expert"),
        P("dp", "expert"),
        P("expert", "dp"),
        P("expert", "dp"),
        P("expert", "dp"),
    )
    return jax.shard_map(
        layer,
        mesh=mesh,
        in_specs=placed,
        out_specs=(
            P("expert", "dp"),
            P("expert", None),
            P("dp", "expert"),
            P("dp", "expert"),
            P("expert", "dp"),
        ),
        check_vma=False,
    )
```

```python
import jax
import jax.numpy as jnp
from jax import lax
from jax.experimental import pallas as pl
from jax.experimental.pallas import tpu as pltpu
from jax.sharding import PartitionSpec as P


BF = jnp.bfloat16
F32 = jnp.float32
CAP = 3
LANES = 128
GRANT = 62 << 20
MIDDLE = 50 << 20
SMALL = 24 << 20
LAST = (((1,), (1,)), ((), ()))
FIRST = (((0,), (0,)), ((), ()))
VMEM = pl.BlockSpec(memory_space=pltpu.VMEM)
SMEM = pl.BlockSpec(memory_space=pltpu.SMEM)
ANY = pl.BlockSpec(memory_space=pl.ANY)


def split3(v):
    hi = v.astype(BF)
    rest = v - hi.astype(F32)
    mid = rest.astype(BF)
    lo = (rest - mid.astype(F32)).astype(BF)
    return hi, mid, lo


def call(kernel, outs, in_specs, args, flops=0, nbytes=0, scratch=(), grant=GRANT, place=VMEM):
    return pl.pallas_call(
        kernel,
        out_shape=outs,
        in_specs=in_specs,
        out_specs=jax.tree.map(lambda _: place, outs),
        scratch_shapes=scratch,
        compiler_params=pltpu.CompilerParams(vmem_limit_bytes=grant),
        cost_estimate=pl.CostEstimate(flops=flops, bytes_accessed=nbytes, transcendentals=0),
    )(*args)


def slot_kernel(live_ref, routes_ref, weights_ref, tokens_ref, grad_ref, send_ref, slots_ref, mix_ref):
    count, quarter = tokens_ref.shape
    experts = slots_ref.shape[0] // CAP
    wide = quarter // LANES
    chunks = 2 * CAP * wide
    expert = lax.broadcasted_iota(jnp.int32, (experts, count), 0)
    live = lax.broadcasted_iota(jnp.int32, (experts, count), 1) < live_ref[0]
    first = (routes_ref[0:1, :] == expert) & live
    second = (routes_ref[1:2, :] == expert) & live
    member = first | second
    before = (
        lax.broadcasted_iota(jnp.int32, (count, count), 0)
        < lax.broadcasted_iota(jnp.int32, (count, count), 1)
    ).astype(BF)
    ahead = jnp.dot(member.astype(BF), before, preferred_element_type=F32)
    weight = jnp.where(first, weights_ref[0:1, :], weights_ref[1:2, :])
    for p in range(CAP):
        chosen = member & (ahead == float(p))
        one_hot = chosen.astype(BF)
        slots_ref[p * experts : (p + 1) * experts, :] = one_hot
        picked = jnp.dot(one_hot, tokens_ref[...], preferred_element_type=F32)
        scaled = jnp.zeros((experts, quarter), F32)
        for piece in split3(jnp.where(chosen, weight, 0.0)):
            scaled = scaled + jnp.dot(piece, grad_ref[...], preferred_element_type=F32)
        for kind, value in enumerate((picked, scaled)):
            for h in range(wide):
                at = (kind * CAP + p) * wide + h
                mix_ref[pl.ds(at, experts, stride=chunks), :] = value[:, h * LANES : (h + 1) * LANES]
    send_ref[...] = mix_ref[...].astype(BF)


def dequant(scale_ref, code_ref, out_ref, base):
    for i in range(scale_ref.shape[0]):
        for j in range(scale_ref.shape[1]):
            lines = slice(i * LANES, (i + 1) * LANES)
            lanes = slice(j * LANES, (j + 1) * LANES)
            out_ref[base + i * LANES : base + (i + 1) * LANES, lanes] = (
                code_ref[lines, lanes].astype(F32) * scale_ref[i, j]
            ).astype(BF)


def dequant_pair_kernel(gs_ref, us_ref, gc_hbm, uc_hbm, out_hbm, code_ref, out_ref, sems):
    half = code_ref.shape[1]
    load = [
        pltpu.make_async_copy(source, code_ref.at[n], sems.at[n])
        for n, source in enumerate((gc_hbm, uc_hbm))
    ]
    for copy in load:
        copy.start()
    save = []
    for n, scale_ref in enumerate((gs_ref, us_ref)):
        load[n].wait()
        dequant(scale_ref, code_ref.at[n], out_ref, n * half)
        lines = slice(n * half, (n + 1) * half)
        save.append(pltpu.make_async_copy(out_ref.at[lines], out_hbm.at[lines], sems.at[2 + n]))
        save[n].start()
    for copy in save:
        copy.wait()


def dequant_one_kernel(ds_ref, dc_ref, out_ref):
    dequant(ds_ref, dc_ref, out_ref, 0)


def row_kernel(got_hbm, wd_hbm, out_hbm, rows_hbm, got_ref, wd_ref, out_ref, rows_ref, mix_ref, sems):
    parts, span, _ = out_ref.shape
    quarter = rows_ref.shape[1] // 2
    groups = rows_ref.shape[0] // CAP
    near = groups // parts
    wide = quarter // LANES
    chunks = 2 * CAP * wide
    load = [
        pltpu.make_async_copy(got_hbm, got_ref, sems.at[0]),
        pltpu.make_async_copy(wd_hbm, wd_ref, sems.at[1]),
    ]
    for copy in load:
        copy.start()
    load[0].wait()
    mix_ref[...] = got_ref[...].astype(F32)

    def unpack(kind, targets):
        for p in range(CAP):
            for h in range(wide):
                at = (kind * CAP + p) * wide + h
                value = mix_ref[pl.ds(at, groups, stride=chunks), :].astype(BF)
                for j in range(parts):
                    for target, lines, lane in targets(j, p * near):
                        target[lines, lane + h * LANES : lane + (h + 1) * LANES] = value[
                            j * near : (j + 1) * near
                        ]

    def whole(j, line, lane):
        return (rows_ref, slice(j * span + line, j * span + line + near), lane)

    unpack(1, lambda j, line: [whole(j, line, quarter)])
    load[1].wait()
    back = lax.dot_general(
        rows_ref[:, quarter:], wd_ref[...], LAST, preferred_element_type=F32
    ).astype(BF)
    unpack(
        0,
        lambda j, line: [whole(j, line, 0), (out_ref.at[j], slice(line, line + near), 0)],
    )
    save = [pltpu.make_async_copy(rows_ref, rows_hbm, sems.at[2])]
    for j in range(parts):
        out_ref[j, :, quarter:] = back[j * span : (j + 1) * span]
        save.append(pltpu.make_async_copy(out_ref.at[j], out_hbm.at[j], sems.at[3 + j]))
    for copy in save:
        copy.start()
    for copy in save:
        copy.wait()


def act_kernel(
    me_ref, part_ref, own_hbm, next_hbm, far_low_hbm, far_high_hbm, prev_hbm, out_ref, act_ref, w_ref, mix_ref, sems
):
    parts, span, _ = part_ref.shape
    near = span // CAP
    quarter = w_ref.shape[1] // 2
    wide = quarter // LANES
    chunks = out_ref.shape[1] // near
    owners = [lax.rem(me_ref[0] + shift, parts) for shift in range(parts)]
    copies = [
        pltpu.make_async_copy(source, target, sems.at[n])
        for n, (source, target) in enumerate(
            (
                (own_hbm, w_ref.at[0]),
                (next_hbm, w_ref.at[1]),
                (prev_hbm, w_ref.at[3]),
                (far_low_hbm, w_ref.at[2, :quarter]),
                (far_high_hbm, w_ref.at[2, quarter:]),
            )
        )
    ]
    for copy in copies:
        copy.start()
    grad_hidden = part_ref[0, :, quarter:].astype(F32)
    for j in range(1, parts):
        grad_hidden = grad_hidden + part_ref[j, :, quarter:].astype(F32)
    gate_pre = up_pre = 0.0
    for shift, needed in ((0, (0,)), (1, (1,)), (3, (2,)), (2, (3, 4))):
        for n in needed:
            copies[n].wait()
        token_rows = part_ref[owners[shift], :, :quarter]
        gate = jnp.dot(token_rows, w_ref[shift, :quarter, :], preferred_element_type=F32)
        gate_pre = gate_pre + gate.astype(BF).astype(F32)
        up = jnp.dot(token_rows, w_ref[shift, quarter:, :], preferred_element_type=F32)
        up_pre = up_pre + up.astype(BF).astype(F32)
    sig = jax.nn.sigmoid(gate_pre)
    activated = gate_pre * sig
    hidden = (activated * up_pre).astype(BF)
    gate_delta = (grad_hidden * up_pre * sig * (1.0 + gate_pre * (1.0 - sig))).astype(BF)
    up_delta = (grad_hidden * activated).astype(BF)
    act_ref[0:span, :] = gate_delta
    act_ref[span : 2 * span, :] = up_delta
    act_ref[2 * span : 3 * span, :] = hidden
    score = jnp.sum(hidden.astype(F32) * grad_hidden, axis=1, keepdims=True)
    lane = lax.broadcasted_iota(jnp.int32, (span, LANES), 1)
    hi, mid, lo = (v.astype(F32) for v in split3(score))
    scores = jnp.where(lane == 0, hi, jnp.where(lane == 1, mid, jnp.where(lane == 2, lo, 0.0)))
    for p in range(CAP):
        mix_ref[pl.ds(CAP * wide + p, near, stride=chunks), :] = scores[p * near : (p + 1) * near]
    for c in range(CAP * wide + CAP, chunks):
        mix_ref[pl.ds(c, near, stride=chunks), :] = jnp.zeros((near, LANES), F32)
    for shift in range(parts):
        grad = lax.dot_general(
            gate_delta, w_ref[shift, :quarter, :], LAST, preferred_element_type=F32
        )
        grad = grad + lax.dot_general(
            up_delta, w_ref[shift, quarter:, :], LAST, preferred_element_type=F32
        )
        for p in range(CAP):
            for h in range(wide):
                mix_ref[pl.ds(p * wide + h, near, stride=chunks), :] = grad[
                    p * near : (p + 1) * near, h * LANES : (h + 1) * LANES
                ]
        out_ref[owners[shift]] = mix_ref[...].astype(BF)


def weight_grad_kernel(me_ref, rows_ref, a0_ref, a1_ref, a2_ref, a3_ref, gg_ref, gu_ref, gd_ref):
    parts = 4
    span = a0_ref.shape[0] // 3
    quarter = gg_ref.shape[0]
    rows, acts = [], []
    for shift, ref in enumerate((a0_ref, a1_ref, a2_ref, a3_ref)):
        owner = lax.rem(me_ref[0] + parts - shift, parts)
        rows.append(rows_ref[pl.ds(pl.multiple_of(owner * span, span), span), :])
        acts.append(ref)
    rows = jnp.concatenate(rows, axis=0)

    def gathered(k):
        return jnp.concatenate([ref[k * span : (k + 1) * span, :] for ref in acts], axis=0)

    token_rows = rows[:, :quarter]
    gg_ref[...] = lax.dot_general(
        token_rows, gathered(0), FIRST, preferred_element_type=F32
    ).astype(BF)
    gu_ref[...] = lax.dot_general(
        token_rows, gathered(1), FIRST, preferred_element_type=F32
    ).astype(BF)
    gd_ref[...] = lax.dot_general(
        gathered(2), rows[:, quarter:], FIRST, preferred_element_type=F32
    ).astype(BF)


def home_kernel(routes_ref, weights_ref, slots_ref, ret_ref, grad_ref, score_ref, mix_ref):
    slots, count = slots_ref.shape
    experts = slots // CAP
    quarter = grad_ref.shape[1]
    wide = quarter // LANES
    chunks = ret_ref.shape[0] // experts
    mix_ref[...] = ret_ref[...].astype(F32)

    def chunk(c):
        return mix_ref[pl.ds(c, experts, stride=chunks), :]

    grad = jnp.zeros((count, quarter), F32)
    expert = lax.broadcasted_iota(jnp.int32, (experts, count), 0)
    scores = [jnp.zeros((1, count), F32)] * 2
    for p in range(CAP):
        one_hot = slots_ref[p * experts : (p + 1) * experts, :]
        block = jnp.concatenate([chunk(p * wide + h).astype(BF) for h in range(wide)], axis=1)
        grad = grad + lax.dot_general(one_hot, block, FIRST, preferred_element_type=F32)
        pieces = chunk(CAP * wide + p)
        picked = one_hot.astype(F32) * (pieces[:, 0:1] + pieces[:, 1:2] + pieces[:, 2:3])
        for k in range(2):
            mine = jnp.where(routes_ref[k : k + 1, :] == expert, picked, 0.0)
            scores[k] = scores[k] + jnp.sum(mine, axis=0, keepdims=True)
    grad_ref[...] = grad.astype(BF)
    for k in range(2):
        score_ref[k : k + 1, :] = scores[k] / weights_ref[k : k + 1, :]


def layer(
    tokens,
    routes,
    route_weights,
    live_tokens,
    gate_codes,
    gate_scales,
    up_codes,
    up_scales,
    down_codes,
    down_scales,
    grad_out,
):
    count, quarter = tokens.shape
    hidden_size = gate_codes.shape[1]
    experts = lax.axis_size("expert")
    parts = lax.axis_size("dp")
    slots = experts * CAP
    span = slots // parts
    shape = jax.ShapeDtypeStruct
    routes_t = routes.T
    weights_t = route_weights.T

    wide = quarter // LANES
    out_chunks = 2 * CAP * wide
    back_chunks = -(-(CAP * wide + CAP) // 8) * 8
    me = lax.axis_index("dp")

    def turn(value, shift):
        return lax.ppermute(value, "dp", [(i, (i + shift) % parts) for i in range(parts)])

    w_own = call(
        dequant_pair_kernel,
        shape((2 * quarter, hidden_size), BF),
        [SMEM] * 2 + [ANY] * 2,
        (gate_scales, up_scales, gate_codes, up_codes),
        flops=2 * quarter * hidden_size,
        nbytes=8 * quarter * hidden_size,
        scratch=[
            pltpu.VMEM((2, quarter, hidden_size), BF),
            pltpu.VMEM((2 * quarter, hidden_size), BF),
            pltpu.SemaphoreType.DMA((4,)),
        ],
        place=ANY,
    )
    w_prev = turn(w_own, 1)
    w_next = turn(w_own, -1)
    send, one_hot = call(
        slot_kernel,
        (shape((experts * out_chunks, LANES), BF), shape((slots, count), BF)),
        [SMEM, VMEM, VMEM, VMEM, VMEM],
        (live_tokens, routes_t, weights_t, tokens, grad_out),
        grant=SMALL,
        flops=2 * slots * count * quarter * 4,
        nbytes=2 * slots * 2 * quarter,
        scratch=[pltpu.VMEM((experts * out_chunks, LANES), F32)],
    )
    got = lax.all_to_all(
        send.reshape(experts, out_chunks, LANES), "expert", split_axis=0, concat_axis=0, tiled=True
    )
    far_low = turn(w_next[:quarter], -1)
    far_high = turn(w_prev[quarter:], 1)
    w_down = call(
        dequant_one_kernel,
        shape(down_codes.shape, BF),
        [SMEM, VMEM],
        (down_scales, down_codes),
        flops=quarter * hidden_size,
        nbytes=4 * quarter * hidden_size,
    )
    part, rows = call(
        row_kernel,
        (shape((parts, span, quarter + hidden_size), BF), shape((slots, 2 * quarter), BF)),
        [ANY] * 2,
        (got.reshape(experts * out_chunks, LANES), w_down),
        flops=2 * slots * quarter * hidden_size,
        nbytes=8 * slots * hidden_size,
        scratch=[
            pltpu.VMEM((experts * out_chunks, LANES), BF),
            pltpu.VMEM((hidden_size, quarter), BF),
            pltpu.VMEM((parts, span, quarter + hidden_size), BF),
            pltpu.VMEM((slots, 2 * quarter), BF),
            pltpu.VMEM((experts * out_chunks, LANES), F32),
            pltpu.SemaphoreType.DMA((3 + parts,)),
        ],
        place=ANY,
    )
    part = lax.all_to_all(part, "dp", split_axis=0, concat_axis=0, tiled=True)
    ret, acts = call(
        act_kernel,
        (
            shape((parts, span // CAP * back_chunks, LANES), BF),
            shape((3 * span, hidden_size), BF),
        ),
        [SMEM, VMEM] + [ANY] * 5,
        (me.reshape(1), part, w_own, w_next, far_low, far_high, w_prev),
        grant=MIDDLE,
        flops=8 * slots * quarter * hidden_size,
        nbytes=16 * quarter * hidden_size,
        scratch=[
            pltpu.VMEM((parts, 2 * quarter, hidden_size), BF),
            pltpu.VMEM((span // CAP * back_chunks, LANES), F32),
            pltpu.SemaphoreType.DMA((5,)),
        ],
    )
    ret = lax.all_to_all(ret, "dp", split_axis=0, concat_axis=0, tiled=True)
    ret, acts = lax.optimization_barrier((ret, acts))
    ret = lax.all_to_all(
        ret.reshape(experts, back_chunks, LANES), "expert", split_axis=0, concat_axis=0, tiled=True
    )
    grad_gate, grad_up, grad_down = call(
        weight_grad_kernel,
        (
            shape((quarter, hidden_size), BF),
            shape((quarter, hidden_size), BF),
            shape((hidden_size, quarter), BF),
        ),
        [SMEM] + [VMEM] * 5,
        (me.reshape(1), rows, acts, turn(acts, 1), turn(acts, 2), turn(acts, 3)),
        grant=SMALL,
        flops=6 * slots * quarter * hidden_size,
        nbytes=16 * slots * hidden_size,
    )
    grad_tokens, grad_weights_t = call(
        home_kernel,
        (shape((count, quarter), BF), shape((2, count), F32)),
        [VMEM] * 4,
        (routes_t, weights_t, one_hot, ret.reshape(experts * back_chunks, LANES)),
        grant=SMALL,
        flops=2 * slots * count * quarter,
        nbytes=2 * slots * quarter,
        scratch=[pltpu.VMEM((experts * back_chunks, LANES), F32)],
    )
    return (grad_tokens, grad_weights_t.T, grad_gate, grad_up, grad_down)


def solution(mesh):
    placed = (
        P("expert", "dp"),
        P("expert", None),
        P("expert", None),
        P("expert"),
        P("dp", "expert"),
        P("dp", "expert"),
        P("dp", "expert"),
        P("dp", "expert"),
        P("expert", "dp"),
        P("expert", "dp"),
        P("expert", "dp"),
    )
    return jax.shard_map(
        layer,
        mesh=mesh,
        in_specs=placed,
        out_specs=(
            P("expert", "dp"),
            P("expert", None),
            P("dp", "expert"),
            P("dp", "expert"),
            P("expert", "dp"),
        ),
        check_vma=False,
    )
```

```python
import jax
import jax.numpy as jnp
from jax import lax
from jax.experimental import pallas as pl
from jax.experimental.pallas import tpu as pltpu
from jax.sharding import PartitionSpec as P


BF = jnp.bfloat16
F32 = jnp.float32
CAP = 3
LANES = 128
GRANT = 62 << 20
MIDDLE = 50 << 20
SMALL = 24 << 20
LAST = (((1,), (1,)), ((), ()))
FIRST = (((0,), (0,)), ((), ()))
VMEM = pl.BlockSpec(memory_space=pltpu.VMEM)
SMEM = pl.BlockSpec(memory_space=pltpu.SMEM)
ANY = pl.BlockSpec(memory_space=pl.ANY)


def split3(v):
    hi = v.astype(BF)
    rest = v - hi.astype(F32)
    mid = rest.astype(BF)
    lo = (rest - mid.astype(F32)).astype(BF)
    return hi, mid, lo


def call(kernel, outs, in_specs, args, flops=0, nbytes=0, scratch=(), grant=GRANT):
    return pl.pallas_call(
        kernel,
        out_shape=outs,
        in_specs=in_specs,
        out_specs=jax.tree.map(lambda _: VMEM, outs),
        scratch_shapes=scratch,
        compiler_params=pltpu.CompilerParams(vmem_limit_bytes=grant),
        cost_estimate=pl.CostEstimate(flops=flops, bytes_accessed=nbytes, transcendentals=0),
    )(*args)


def slot_kernel(live_ref, routes_ref, weights_ref, tokens_ref, grad_ref, send_ref, slots_ref, mix_ref):
    count, quarter = tokens_ref.shape
    experts = slots_ref.shape[0] // CAP
    wide = quarter // LANES
    chunks = 2 * CAP * wide
    expert = lax.broadcasted_iota(jnp.int32, (experts, count), 0)
    live = lax.broadcasted_iota(jnp.int32, (experts, count), 1) < live_ref[0]
    first = (routes_ref[0:1, :] == expert) & live
    second = (routes_ref[1:2, :] == expert) & live
    member = first | second
    before = (
        lax.broadcasted_iota(jnp.int32, (count, count), 0)
        < lax.broadcasted_iota(jnp.int32, (count, count), 1)
    ).astype(BF)
    ahead = jnp.dot(member.astype(BF), before, preferred_element_type=F32)
    weight = jnp.where(first, weights_ref[0:1, :], weights_ref[1:2, :])
    for p in range(CAP):
        chosen = member & (ahead == float(p))
        one_hot = chosen.astype(BF)
        slots_ref[p * experts : (p + 1) * experts, :] = one_hot
        picked = jnp.dot(one_hot, tokens_ref[...], preferred_element_type=F32)
        scaled = jnp.zeros((experts, quarter), F32)
        for piece in split3(jnp.where(chosen, weight, 0.0)):
            scaled = scaled + jnp.dot(piece, grad_ref[...], preferred_element_type=F32)
        for kind, value in enumerate((picked, scaled)):
            for h in range(wide):
                at = (kind * CAP + p) * wide + h
                mix_ref[pl.ds(at, experts, stride=chunks), :] = value[:, h * LANES : (h + 1) * LANES]
    send_ref[...] = mix_ref[...].astype(BF)


def dequant(scale_ref, code_ref, out_ref, base):
    for i in range(scale_ref.shape[0]):
        for j in range(scale_ref.shape[1]):
            lines = slice(i * LANES, (i + 1) * LANES)
            lanes = slice(j * LANES, (j + 1) * LANES)
            out_ref[base + i * LANES : base + (i + 1) * LANES, lanes] = (
                code_ref[lines, lanes].astype(F32) * scale_ref[i, j]
            ).astype(BF)


def dequant_pair_kernel(gs_ref, us_ref, gc_ref, uc_ref, out_ref):
    dequant(gs_ref, gc_ref, out_ref, 0)
    dequant(us_ref, uc_ref, out_ref, gc_ref.shape[0])


def dequant_one_kernel(ds_ref, dc_ref, out_ref):
    dequant(ds_ref, dc_ref, out_ref, 0)


def unpack(got_ref, mix_ref, rows_ref, parts):
    slots, width = rows_ref.shape
    groups = slots // CAP
    near = groups // parts
    chunks = CAP * width // LANES
    wide = width // (2 * LANES)
    mix_ref[...] = got_ref[...].astype(F32)
    for kind in range(2):
        for p in range(CAP):
            for h in range(wide):
                at = (kind * CAP + p) * wide + h
                lane = (kind * wide + h) * LANES
                value = mix_ref[pl.ds(at, groups, stride=chunks), :].astype(BF)
                for j in range(parts):
                    line = (j * CAP + p) * near
                    rows_ref[line : line + near, lane : lane + LANES] = value[
                        j * near : (j + 1) * near
                    ]


def row_kernel(got_ref, wd_ref, out_ref, rows_ref, mix_ref):
    parts, span, _ = out_ref.shape
    quarter = rows_ref.shape[1] // 2
    unpack(got_ref, mix_ref, rows_ref, parts)
    back = lax.dot_general(
        rows_ref[:, quarter:], wd_ref[...], LAST, preferred_element_type=F32
    ).astype(BF)
    for j in range(parts):
        lines = slice(j * span, (j + 1) * span)
        out_ref[j, :, :quarter] = rows_ref[lines, :quarter]
        out_ref[j, :, quarter:] = back[lines]


def act_kernel(
    me_ref, part_ref, own_hbm, next_hbm, far_low_hbm, far_high_hbm, prev_hbm, out_ref, act_ref, w_ref, mix_ref, sems
):
    parts, span, _ = part_ref.shape
    near = span // CAP
    quarter = w_ref.shape[1] // 2
    wide = quarter // LANES
    chunks = out_ref.shape[1] // near
    owners = [lax.rem(me_ref[0] + shift, parts) for shift in range(parts)]
    copies = [
        pltpu.make_async_copy(source, target, sems.at[n])
        for n, (source, target) in enumerate(
            (
                (own_hbm, w_ref.at[0]),
                (next_hbm, w_ref.at[1]),
                (prev_hbm, w_ref.at[3]),
                (far_low_hbm, w_ref.at[2, :quarter]),
                (far_high_hbm, w_ref.at[2, quarter:]),
            )
        )
    ]
    for copy in copies:
        copy.start()
    grad_hidden = part_ref[0, :, quarter:].astype(F32)
    for j in range(1, parts):
        grad_hidden = grad_hidden + part_ref[j, :, quarter:].astype(F32)
    gate_pre = up_pre = 0.0
    for shift, needed in ((0, (0,)), (1, (1,)), (3, (2,)), (2, (3, 4))):
        for n in needed:
            copies[n].wait()
        token_rows = part_ref[owners[shift], :, :quarter]
        gate = jnp.dot(token_rows, w_ref[shift, :quarter, :], preferred_element_type=F32)
        gate_pre = gate_pre + gate.astype(BF).astype(F32)
        up = jnp.dot(token_rows, w_ref[shift, quarter:, :], preferred_element_type=F32)
        up_pre = up_pre + up.astype(BF).astype(F32)
    sig = jax.nn.sigmoid(gate_pre)
    activated = gate_pre * sig
    hidden = (activated * up_pre).astype(BF)
    gate_delta = (grad_hidden * up_pre * sig * (1.0 + gate_pre * (1.0 - sig))).astype(BF)
    up_delta = (grad_hidden * activated).astype(BF)
    act_ref[0:span, :] = gate_delta
    act_ref[span : 2 * span, :] = up_delta
    act_ref[2 * span : 3 * span, :] = hidden
    score = jnp.sum(hidden.astype(F32) * grad_hidden, axis=1, keepdims=True)
    lane = lax.broadcasted_iota(jnp.int32, (span, LANES), 1)
    hi, mid, lo = (v.astype(F32) for v in split3(score))
    scores = jnp.where(lane == 0, hi, jnp.where(lane == 1, mid, jnp.where(lane == 2, lo, 0.0)))
    for p in range(CAP):
        mix_ref[pl.ds(CAP * wide + p, near, stride=chunks), :] = scores[p * near : (p + 1) * near]
    for c in range(CAP * wide + CAP, chunks):
        mix_ref[pl.ds(c, near, stride=chunks), :] = jnp.zeros((near, LANES), F32)
    for shift in range(parts):
        grad = lax.dot_general(
            gate_delta, w_ref[shift, :quarter, :], LAST, preferred_element_type=F32
        )
        grad = grad + lax.dot_general(
            up_delta, w_ref[shift, quarter:, :], LAST, preferred_element_type=F32
        )
        for p in range(CAP):
            for h in range(wide):
                mix_ref[pl.ds(p * wide + h, near, stride=chunks), :] = grad[
                    p * near : (p + 1) * near, h * LANES : (h + 1) * LANES
                ]
        out_ref[owners[shift]] = mix_ref[...].astype(BF)


def weight_grad_kernel(
    me_ref, got_ref, a0_ref, a1_ref, a2_ref, a3_ref, gg_ref, gu_ref, gd_ref, rows_ref, mix_ref
):
    parts = 4
    unpack(got_ref, mix_ref, rows_ref, parts)
    span = a0_ref.shape[0] // 3
    quarter = gg_ref.shape[0]
    rows, acts = [], []
    for shift, ref in enumerate((a0_ref, a1_ref, a2_ref, a3_ref)):
        owner = lax.rem(me_ref[0] + parts - shift, parts)
        rows.append(rows_ref[pl.ds(pl.multiple_of(owner * span, span), span), :])
        acts.append(ref)
    rows = jnp.concatenate(rows, axis=0)

    def gathered(k):
        return jnp.concatenate([ref[k * span : (k + 1) * span, :] for ref in acts], axis=0)

    token_rows = rows[:, :quarter]
    gg_ref[...] = lax.dot_general(
        token_rows, gathered(0), FIRST, preferred_element_type=F32
    ).astype(BF)
    gu_ref[...] = lax.dot_general(
        token_rows, gathered(1), FIRST, preferred_element_type=F32
    ).astype(BF)
    gd_ref[...] = lax.dot_general(
        gathered(2), rows[:, quarter:], FIRST, preferred_element_type=F32
    ).astype(BF)


def home_kernel(routes_ref, weights_ref, slots_ref, ret_ref, grad_ref, score_ref, mix_ref):
    slots, count = slots_ref.shape
    experts = slots // CAP
    quarter = grad_ref.shape[1]
    wide = quarter // LANES
    chunks = ret_ref.shape[0] // experts
    mix_ref[...] = ret_ref[...].astype(F32)

    def chunk(c):
        return mix_ref[pl.ds(c, experts, stride=chunks), :]

    grad = jnp.zeros((count, quarter), F32)
    expert = lax.broadcasted_iota(jnp.int32, (experts, count), 0)
    scores = [jnp.zeros((1, count), F32)] * 2
    for p in range(CAP):
        one_hot = slots_ref[p * experts : (p + 1) * experts, :]
        block = jnp.concatenate([chunk(p * wide + h).astype(BF) for h in range(wide)], axis=1)
        grad = grad + lax.dot_general(one_hot, block, FIRST, preferred_element_type=F32)
        pieces = chunk(CAP * wide + p)
        picked = one_hot.astype(F32) * (pieces[:, 0:1] + pieces[:, 1:2] + pieces[:, 2:3])
        for k in range(2):
            mine = jnp.where(routes_ref[k : k + 1, :] == expert, picked, 0.0)
            scores[k] = scores[k] + jnp.sum(mine, axis=0, keepdims=True)
    grad_ref[...] = grad.astype(BF)
    for k in range(2):
        score_ref[k : k + 1, :] = scores[k] / weights_ref[k : k + 1, :]


def layer(
    tokens,
    routes,
    route_weights,
    live_tokens,
    gate_codes,
    gate_scales,
    up_codes,
    up_scales,
    down_codes,
    down_scales,
    grad_out,
):
    count, quarter = tokens.shape
    hidden_size = gate_codes.shape[1]
    experts = lax.axis_size("expert")
    parts = lax.axis_size("dp")
    slots = experts * CAP
    span = slots // parts
    shape = jax.ShapeDtypeStruct
    routes_t = routes.T
    weights_t = route_weights.T

    wide = quarter // LANES
    out_chunks = 2 * CAP * wide
    back_chunks = -(-(CAP * wide + CAP) // 8) * 8
    me = lax.axis_index("dp")

    def turn(value, shift):
        return lax.ppermute(value, "dp", [(i, (i + shift) % parts) for i in range(parts)])

    w_own = call(
        dequant_pair_kernel,
        shape((2 * quarter, hidden_size), BF),
        [SMEM] * 2 + [VMEM] * 2,
        (gate_scales, up_scales, gate_codes, up_codes),
        flops=2 * quarter * hidden_size,
        nbytes=8 * quarter * hidden_size,
    )
    w_prev = turn(w_own, 1)
    w_next = turn(w_own, -1)
    send, one_hot = call(
        slot_kernel,
        (shape((experts * out_chunks, LANES), BF), shape((slots, count), BF)),
        [SMEM, VMEM, VMEM, VMEM, VMEM],
        (live_tokens, routes_t, weights_t, tokens, grad_out),
        grant=SMALL,
        flops=2 * slots * count * quarter * 4,
        nbytes=2 * slots * 2 * quarter,
        scratch=[pltpu.VMEM((experts * out_chunks, LANES), F32)],
    )
    got = lax.all_to_all(
        send.reshape(experts, out_chunks, LANES),
        "expert",
        split_axis=0,
        concat_axis=0,
        tiled=True,
    )
    far_low = turn(w_next[:quarter], -1)
    far_high = turn(w_prev[quarter:], 1)
    w_down = call(
        dequant_one_kernel,
        shape(down_codes.shape, BF),
        [SMEM, VMEM],
        (down_scales, down_codes),
        grant=MIDDLE,
        flops=quarter * hidden_size,
        nbytes=4 * quarter * hidden_size,
    )
    got = got.reshape(experts * out_chunks, LANES)
    unpacking = [
        pltpu.VMEM((slots, 2 * quarter), BF),
        pltpu.VMEM((experts * out_chunks, LANES), F32),
    ]
    part = call(
        row_kernel,
        shape((parts, span, quarter + hidden_size), BF),
        [VMEM] * 2,
        (got, w_down),
        grant=MIDDLE,
        flops=2 * slots * quarter * hidden_size,
        nbytes=8 * slots * hidden_size,
        scratch=unpacking,
    )
    part = lax.all_to_all(part, "dp", split_axis=0, concat_axis=0, tiled=True)
    ret, acts = call(
        act_kernel,
        (
            shape((parts, span // CAP * back_chunks, LANES), BF),
            shape((3 * span, hidden_size), BF),
        ),
        [SMEM, VMEM] + [ANY] * 5,
        (me.reshape(1), part, w_own, w_next, far_low, far_high, w_prev),
        grant=MIDDLE,
        flops=8 * slots * quarter * hidden_size,
        nbytes=16 * quarter * hidden_size,
        scratch=[
            pltpu.VMEM((parts, 2 * quarter, hidden_size), BF),
            pltpu.VMEM((span // CAP * back_chunks, LANES), F32),
            pltpu.SemaphoreType.DMA((5,)),
        ],
    )
    ret = lax.all_to_all(ret, "dp", split_axis=0, concat_axis=0, tiled=True)
    ret, acts = lax.optimization_barrier((ret, acts))
    ret = lax.all_to_all(
        ret.reshape(experts, back_chunks, LANES), "expert", split_axis=0, concat_axis=0, tiled=True
    )
    grad_gate, grad_up, grad_down = call(
        weight_grad_kernel,
        (
            shape((quarter, hidden_size), BF),
            shape((quarter, hidden_size), BF),
            shape((hidden_size, quarter), BF),
        ),
        [SMEM] + [VMEM] * 5,
        (me.reshape(1), got, acts, turn(acts, 1), turn(acts, 2), turn(acts, 3)),
        grant=SMALL,
        flops=6 * slots * quarter * hidden_size,
        nbytes=16 * slots * hidden_size,
        scratch=unpacking,
    )
    grad_tokens, grad_weights_t = call(
        home_kernel,
        (shape((count, quarter), BF), shape((2, count), F32)),
        [VMEM] * 4,
        (routes_t, weights_t, one_hot, ret.reshape(experts * back_chunks, LANES)),
        grant=SMALL,
        flops=2 * slots * count * quarter,
        nbytes=2 * slots * quarter,
        scratch=[pltpu.VMEM((experts * back_chunks, LANES), F32)],
    )
    return (grad_tokens, grad_weights_t.T, grad_gate, grad_up, grad_down)


def solution(mesh):
    placed = (
        P("expert", "dp"),
        P("expert", None),
        P("expert", None),
        P("expert"),
        P("dp", "expert"),
        P("dp", "expert"),
        P("dp", "expert"),
        P("dp", "expert"),
        P("expert", "dp"),
        P("expert", "dp"),
        P("expert", "dp"),
    )
    return jax.shard_map(
        layer,
        mesh=mesh,
        in_specs=placed,
        out_specs=(
            P("expert", "dp"),
            P("expert", None),
            P("dp", "expert"),
            P("dp", "expert"),
            P("expert", "dp"),
        ),
        check_vma=False,
    )
```
